256 devices in a mesh: ap: 32 (over x, z_hi, core), pass: 8 (over y, z_lo).
Axes of the slice: x: 4, y: 4, z: 8 (z_hi: 4, z_lo: 2; z = z_hi * 2 + z_lo), core: 2. Of those that a mesh axis runs over, the one named last changes fastest.
Arguments:
- echo_record: bfloat16 [2, 64, 2048, 512], P(None, 'pass', 'ap'), may hold values from -6 to 6
- along_track_kernel: bfloat16 [2, 1024, 2048], P(None, None, 'ap'), may hold values from -0.1875 to 0.1875
- slant_distance_kernel: bfloat16 [2, 512, 256], replicated, may hold values from -0.1875 to 0.1875
- vertical_lags: int32 [64], P('pass'), may hold values from 0 to 64
- lateral_lags: int32 [64], P('pass'), may hold values from 0 to 32
- orbit_source_survey: int32 [64], replicated, may hold values from 0 to 63, each once
- normal_spacings: float32 [64], replicated, may hold values from -1 to 1
Outputs:
- profile: float32 [2, 1024, 256, 512], P(None, ('ap', 'pass'))
The draws below stay inside these ranges and needn't reach their ends.
All inputs are finite; a program needn't handle non-finite values.
Results may differ from the reference program's by a relative error of at most 0.02.
Values may be sent and summed in bfloat16 or wider, within the bound.
No kernel may reach another device: no remote copies, remote signals or barrier semaphores. Data moves between devices by JAX's collectives and lax.ppermute only.
A program may use at most 128 MiB of HBM per device.

```python
import jax
import jax.numpy as jnp
from jax import lax

ORBIT_SUM = 64
PULSES = 2048
FREQS = 512
ROWS = 1024
COLS = 256
HEIGHT_CELLS = 512
ITERS = 4
COL_MAX = 32
OFF_MAX = 64


def touch_ends(entries, rng, low, largest):
    index_at = [jax.random.randint(jax.random.fold_in(rng, axis), (), 0, length) for axis, length in enumerate(entries.shape)]
    widest = entries.shape.index(max(entries.shape))
    neighbour = index_at[:widest] + [(index_at[widest] + 1) % entries.shape[widest]] + index_at[widest + 1:]
    return entries.at[tuple(index_at)].set(low).at[tuple(neighbour)].set(largest)


def raised(entries, stream_key, source, target, blocks, factor):
    def block_of(position):
        return (jnp.arange(entries.shape[position]) // (entries.shape[position] // blocks)).reshape((-1,) + (1,) * (entries.ndim - 1 - position))

    near = jax.random.permutation(stream_key, blocks)[block_of(target)]
    other_side = (block_of(target) + blocks // 2) % blocks
    return jnp.where((block_of(source) == near) | (block_of(source) == other_side), factor * entries, entries)


def level_of(rng, dims, cuts, least, largest):
    loudness = 1.0
    for position, parts in cuts:
        draws = jax.random.uniform(jax.random.fold_in(jax.random.fold_in(rng, 6), position), (parts,), jnp.float32, least / len(cuts), largest / len(cuts))
        loudness = loudness * jnp.repeat(jnp.exp(draws), dims[position] // parts).reshape((-1,) + (1,) * (len(dims) - 1 - position))
    return loudness


def normal_values(own_key, extent, width, reach, shards=(), kind=jnp.bfloat16):
    result = jax.random.normal(own_key, extent, jnp.float32) * width
    if len(shards) > 0:
        result = level_of(own_key, extent, shards, -0.22, 0.18) * result
    return jnp.clip(result, min=-reach, max=reach).astype(kind)


def bell_draw_with(key, shape, spread, bound, split, heavy, held_as=jnp.bfloat16):
    array = spread * jax.random.normal(key, shape, jnp.float32)
    if split:
        array = array * level_of(key, shape, split, -0.22, 0.18)
    return jnp.clip(raised(array, jax.random.fold_in(key, 3), *heavy), -bound, bound).astype(held_as)


def setup_inputs(seed: int = 0) -> dict:
    key_of = jax.random.split(jax.random.key(seed), 8)
    return {
        "echo_record": normal_values(key_of[0], (2, ORBIT_SUM, PULSES, FREQS), 1.0, 6.0, ((1, 8), (2, 32))),
        "along_track_kernel": bell_draw_with(key_of[1], (2, ROWS, PULSES), (2 * PULSES) ** -0.5, 0.1875, ((2, 32),), (2, 1, 32, 2.75)),
        "slant_distance_kernel": normal_values(key_of[2], (2, FREQS, COLS), (2 * FREQS) ** -0.5, 0.1875),
        "vertical_lags": touch_ends(jax.random.randint(key_of[3], (ORBIT_SUM,), 0, OFF_MAX + 1), jax.random.fold_in(key_of[3], 1), 0, OFF_MAX).astype(jnp.int32),
        "lateral_lags": touch_ends(jax.random.randint(key_of[4], (ORBIT_SUM,), 0, COL_MAX + 1), jax.random.fold_in(key_of[4], 1), 0, COL_MAX).astype(jnp.int32),
        "orbit_source_survey": jax.random.permutation(key_of[5], ORBIT_SUM).astype(jnp.int32),
        "normal_spacings": jnp.clip(jax.random.uniform(key_of[6], (ORBIT_SUM,), jnp.float32, -1.0, 1.0), -1.0, 1.0),
    }


shrink_level = 0.1


def phasor_dictionary(normal_spacings, orbit_source_survey, height_cell_number):
    chosen_height_cells = normal_spacings[orbit_source_survey]
    orbit_start_positions = jnp.arange(height_cell_number).astype(normal_spacings.dtype) - height_cell_number // 2
    phases = jnp.pi * chosen_height_cells[:, None] * orbit_start_positions[None, :]
    return jnp.cos(phases), jnp.sin(phases)


def shrink_steps(obs_re, obs_im, inphase_phasor_part, quadrature_phasor_part):
    passes = inphase_phasor_part.shape[0]
    height_cell_number = inphase_phasor_part.shape[1]
    precise = lax.Precision.HIGHEST
    prof_re = jnp.zeros((obs_re.shape[0], height_cell_number), jnp.float32)
    prof_im = jnp.zeros((obs_re.shape[0], height_cell_number), jnp.float32)
    for sweep_index in range(ITERS):
        if sweep_index == 0:
            resid_re = obs_re
            resid_im = obs_im
        else:
            pred_re = jnp.dot(prof_re, inphase_phasor_part.T, precision=precise) - jnp.dot(prof_im, quadrature_phasor_part.T, precision=precise)
            pred_im = jnp.dot(prof_re, quadrature_phasor_part.T, precision=precise) + jnp.dot(prof_im, inphase_phasor_part.T, precision=precise)
            resid_re = obs_re - pred_re / height_cell_number
            resid_im = obs_im - pred_im / height_cell_number
        grad_re = jnp.dot(resid_re, inphase_phasor_part, precision=precise) + jnp.dot(resid_im, quadrature_phasor_part, precision=precise)
        grad_im = jnp.dot(resid_im, inphase_phasor_part, precision=precise) - jnp.dot(resid_re, quadrature_phasor_part, precision=precise)
        moved_re = prof_re + grad_re / passes
        moved_im = prof_im + grad_im / passes
        prof_re = moved_re - jnp.clip(moved_re, -shrink_level, shrink_level)
        prof_im = moved_im - jnp.clip(moved_im, -shrink_level, shrink_level)
    return prof_re, prof_im


def reference(echo_record, along_track_kernel, slant_distance_kernel, vertical_lags, lateral_lags, orbit_source_survey, normal_spacings):
    def form_pass(inputs):
        planes, row_offset, col_offset = inputs
        focus_re = (jnp.dot(planes[0], slant_distance_kernel[0], preferred_element_type=jnp.float32)
                    - jnp.dot(planes[1], slant_distance_kernel[1], preferred_element_type=jnp.float32)).astype(jnp.bfloat16)
        focus_im = (jnp.dot(planes[0], slant_distance_kernel[1], preferred_element_type=jnp.float32)
                    + jnp.dot(planes[1], slant_distance_kernel[0], preferred_element_type=jnp.float32)).astype(jnp.bfloat16)
        image_re = (jnp.dot(along_track_kernel[0], focus_re, preferred_element_type=jnp.float32)
                    - jnp.dot(along_track_kernel[1], focus_im, preferred_element_type=jnp.float32))
        image_im = (jnp.dot(along_track_kernel[0], focus_im, preferred_element_type=jnp.float32)
                    + jnp.dot(along_track_kernel[1], focus_re, preferred_element_type=jnp.float32))
        stacked = jnp.stack([image_re, image_im])
        padded = jnp.pad(stacked, ((0, 0), (OFF_MAX, 0), (COL_MAX, 0)))
        starts = (jnp.int32(0), (OFF_MAX - row_offset).astype(jnp.int32), (COL_MAX - col_offset).astype(jnp.int32))
        return lax.dynamic_slice(padded, starts, (2, ROWS, COLS)).astype(jnp.bfloat16)

    aligned = lax.map(form_pass, (jnp.moveaxis(echo_record, 1, 0), vertical_lags, lateral_lags))
    inphase_phasor_part, quadrature_phasor_part = phasor_dictionary(normal_spacings, orbit_source_survey, HEIGHT_CELLS)
    blocks = 16
    block_rows = ROWS // blocks
    grouped = jnp.moveaxis(aligned.reshape(ORBIT_SUM, 2, blocks, block_rows * COLS), 2, 0)

    def solve_block(portion):
        values = portion.astype(jnp.float32)
        prof_re, prof_im = shrink_steps(values[:, 0].T, values[:, 1].T, inphase_phasor_part, quadrature_phasor_part)
        return jnp.stack([prof_re, prof_im])

    solved = lax.map(solve_block, grouped)
    return jnp.moveaxis(solved, 1, 0).reshape(2, ROWS, COLS, HEIGHT_CELLS)
```

```python
import jax
import jax.numpy as jnp
from jax import lax
from jax.experimental import pallas as pl
from jax.experimental.pallas import tpu as pltpu
from jax.sharding import Mesh, PartitionSpec as P

BINS = 512
ITERS = 4
ROW_MAX = 64
LEVEL = 0.1

VMEM = pl.BlockSpec(memory_space=pltpu.VMEM)
SMEM = pl.BlockSpec(memory_space=pltpu.SMEM)


def dot(a, b, ca, cb):
    return lax.dot_general(a, b, (((ca,), (cb,)), ((), ())), preferred_element_type=jnp.float32)


def focus_kernel(lat_ref, echo_ref, kern_ref, out_ref):
    passes, _, pulses, cols = out_ref.shape
    kr = kern_ref[0]
    ki = kern_ref[1]
    col = lax.broadcasted_iota(jnp.int32, (pulses, cols), 1)
    for q in range(passes):
        er = echo_ref[0, q]
        ei = echo_ref[1, q]
        lag = lat_ref[q]
        keep = col >= lag
        fr = dot(er, kr, 1, 0) - dot(ei, ki, 1, 0)
        fi = dot(er, ki, 1, 0) + dot(ei, kr, 1, 0)
        fr = jnp.where(keep, pltpu.roll(fr, lag, 1), 0.0)
        fi = jnp.where(keep, pltpu.roll(fi, lag, 1), 0.0)
        out_ref[q, 0] = fr.astype(out_ref.dtype)
        out_ref[q, 1] = fi.astype(out_ref.dtype)


def image_kernel(q_ref, ver_ref, at_ref, f_ref, out_ref, re_ref, im_ref):
    parts, _, pulses, rows = at_ref.shape
    cols = f_ref.shape[3]
    lag = ver_ref[q_ref[0]]
    fr = f_ref[:, 0].reshape(parts * pulses, cols)
    fi = f_ref[:, 1].reshape(parts * pulses, cols)
    re_ref[0:ROW_MAX] = jnp.zeros((ROW_MAX, cols), jnp.float32)
    im_ref[0:ROW_MAX] = jnp.zeros((ROW_MAX, cols), jnp.float32)
    step = 256
    for r0 in range(0, rows, step):
        ar = at_ref[:, 0, :, r0 : r0 + step].reshape(parts * pulses, step)
        ai = at_ref[:, 1, :, r0 : r0 + step].reshape(parts * pulses, step)
        re_ref[ROW_MAX + r0 : ROW_MAX + r0 + step] = dot(ar, fr, 0, 0) - dot(ai, fi, 0, 0)
        im_ref[ROW_MAX + r0 : ROW_MAX + r0 + step] = dot(ar, fi, 0, 0) + dot(ai, fr, 0, 0)
    block = 128
    start = ROW_MAX - lag
    base = pl.multiple_of(start // 8 * 8, 8)
    rest = start - base

    def shifted(ref, r0):
        wide = ref[pl.ds(base + r0, block + 8)]
        return pltpu.roll(wide, block + 8 - rest, 0)[:block]

    sub = lax.broadcasted_iota(jnp.int32, (block // 8, 8, cols), 1)
    for r0 in range(0, rows, block):
        re = shifted(re_ref, r0).reshape(block // 8, 8, cols)
        im = shifted(im_ref, r0).reshape(block // 8, 8, cols)
        first = jnp.where(sub < 4, re, pltpu.roll(im, 4, 1))
        second = jnp.where(sub < 4, pltpu.roll(re, 4, 1), im)
        both = jnp.stack([first, second], axis=1).reshape(2 * block, cols)
        out_ref[2 * r0 : 2 * r0 + 2 * block] = both.astype(out_ref.dtype)


def recover_kernel(img_ref, g_ref, h_ref, out_ref, y_ref):
    i = pl.program_id(0)
    xs, parts, others, eight, cols = img_ref.shape
    passes = xs * others

    @pl.when(i == 0)
    def _():
        for x in range(xs):
            acc = img_ref[x, 0].astype(jnp.float32)
            for z in range(1, parts):
                acc = acc + img_ref[x, z].astype(jnp.float32)
            acc = acc.reshape(others * eight, cols)
            for c in range(cols // 128):
                y_ref[c, x * others * eight : (x + 1) * others * eight] = acc[:, c * 128 : c * 128 + 128]

    g = g_ref[...]
    h = h_ref[...]
    y = jnp.concatenate(
        [
            jnp.concatenate(
                [
                    y_ref.at[c][pl.ds(i, passes, stride=eight), :],
                    y_ref.at[c][pl.ds(eight // 2 + i, passes, stride=eight), :],
                ],
                axis=0,
            ).T
            for c in range(cols // 128)
        ],
        axis=0,
    )
    yb = y.astype(jnp.bfloat16)
    yt = yb.astype(jnp.float32)
    v = dot(yb, g, 1, 0)
    u = v - jnp.clip(v, -LEVEL, LEVEL)
    for _ in range(ITERS - 1):
        resid = yt - dot(u.astype(jnp.bfloat16), h, 1, 0)
        v = u + dot(resid.astype(jnp.bfloat16), g, 1, 0)
        u = v - jnp.clip(v, -LEVEL, LEVEL)
    out_ref[0, 0] = u[:, :BINS]
    out_ref[1, 0] = u[:, BINS:]


def steering(normal_spacings, source):
    chosen = jnp.sum(
        jnp.where(
            source[:, None] == jnp.arange(normal_spacings.shape[0], dtype=jnp.int32)[None, :],
            normal_spacings[None, :],
            0.0,
        ),
        axis=1,
    )
    bins = jnp.arange(BINS).astype(normal_spacings.dtype) - BINS // 2
    phases = jnp.pi * chosen[:, None] * bins[None, :]
    return jnp.cos(phases), jnp.sin(phases)


def body(echo, along, slant, vertical, lateral, survey, spacings):
    passes = vertical.shape[0]
    pulses = along.shape[2]
    rows = along.shape[1]
    cols = slant.shape[2]
    total = survey.shape[0]
    near = ("x", "c")
    every = ("x", "zh", "c", "y", "zl")
    bf = jnp.bfloat16

    at = lax.all_gather(jnp.transpose(along, (0, 2, 1)), near, axis=0)
    focus = pl.pallas_call(
        focus_kernel,
        out_shape=jax.ShapeDtypeStruct((passes, 2, pulses, cols), bf),
        in_specs=[SMEM, VMEM, VMEM],
        out_specs=VMEM,
        name="focus",
    )(lateral, echo, slant)
    focus = lax.all_to_all(focus, near, 0, 0, tiled=True)
    mine = (lax.axis_index("x") * 2 + lax.axis_index("c")).astype(jnp.int32).reshape(1)
    image = pl.pallas_call(
        image_kernel,
        out_shape=jax.ShapeDtypeStruct((2 * rows, cols), bf),
        in_specs=[SMEM, SMEM, VMEM, VMEM],
        out_specs=VMEM,
        scratch_shapes=[pltpu.VMEM((rows + ROW_MAX + 8, cols), jnp.float32)] * 2,
        compiler_params=pltpu.CompilerParams(vmem_limit_bytes=40 << 20),
        name="image",
    )(mine, vertical, at, focus)
    image = lax.all_to_all(image, every, 0, 0, tiled=True)

    order = survey.reshape(total // passes, passes).T.reshape(total)
    cos, sin = steering(spacings, order)
    g = jnp.concatenate(
        [jnp.concatenate([cos, -sin], axis=1), jnp.concatenate([sin, cos], axis=1)], axis=0
    )
    gb = (g / total).astype(bf)
    hb = (g.T / BINS).astype(bf)
    nx = lax.axis_size("x")
    nz = lax.axis_size("zh")
    own = 4
    image = image.reshape(nx, nz, total // nx, 2 * own, cols)
    return pl.pallas_call(
        recover_kernel,
        grid=(own,),
        out_shape=jax.ShapeDtypeStruct((2, own, cols, BINS), jnp.float32),
        in_specs=[
            pl.BlockSpec(image.shape, lambda i: (0, 0, 0, 0, 0)),
            pl.BlockSpec(gb.shape, lambda i: (0, 0)),
            pl.BlockSpec(hb.shape, lambda i: (0, 0)),
        ],
        out_specs=pl.BlockSpec((2, 1, cols, BINS), lambda i: (0, i, 0, 0)),
        scratch_shapes=[pltpu.VMEM((cols // 128, total * 2 * own, 128), jnp.float32)],
        compiler_params=pltpu.CompilerParams(vmem_limit_bytes=40 << 20),
        name="recover",
    )(image, gb, hb)


def solution(mesh):
    fine = Mesh(mesh.devices.reshape(4, 4, 2, 4, 2), ("x", "zh", "c", "y", "zl"))
    ap = ("x", "zh", "c")
    group = ("y", "zl")
    return jax.shard_map(
        body,
        mesh=fine,
        in_specs=(
            P(None, group, ap, None),
            P(None, None, ap),
            P(),
            P(group),
            P(group),
            P(),
            P(),
        ),
        out_specs=P(None, ap + group, None, None),
        check_vma=False,
    )
```

```python
import jax
import jax.numpy as jnp
from jax import lax
from jax.experimental import pallas as pl
from jax.experimental.pallas import tpu as pltpu
from jax.sharding import Mesh, PartitionSpec as P

BINS = 512
ITERS = 4
ROW_MAX = 64
LEVEL = 0.1

VMEM = pl.BlockSpec(memory_space=pltpu.VMEM)
SMEM = pl.BlockSpec(memory_space=pltpu.SMEM)


def dot(a, b, ca, cb):
    return lax.dot_general(a, b, (((ca,), (cb,)), ((), ())), preferred_element_type=jnp.float32)


def focus_kernel(lat_ref, echo_ref, kern_ref, out_ref):
    passes, _, pulses, cols = out_ref.shape
    kr = kern_ref[0]
    ki = kern_ref[1]
    col = lax.broadcasted_iota(jnp.int32, (pulses, cols), 1)
    for q in range(passes):
        er = echo_ref[0, q]
        ei = echo_ref[1, q]
        lag = lat_ref[q]
        keep = col >= lag
        fr = dot(er, kr, 1, 0) - dot(ei, ki, 1, 0)
        fi = dot(er, ki, 1, 0) + dot(ei, kr, 1, 0)
        fr = jnp.where(keep, pltpu.roll(fr, lag, 1), 0.0)
        fi = jnp.where(keep, pltpu.roll(fi, lag, 1), 0.0)
        out_ref[q, 0] = fr.astype(out_ref.dtype)
        out_ref[q, 1] = fi.astype(out_ref.dtype)


def image_kernel(order_ref, ver_ref, *refs):
    f_ref, out_ref, re_ref, im_ref = refs[-4:]
    at_refs = refs[:-4]
    _, _, _, cols = f_ref.shape
    rows = at_refs[0].shape[2]
    lag = ver_ref[order_ref[0]]
    fr = jnp.concatenate([f_ref[order_ref[k], 0] for k in range(len(at_refs))], axis=0)
    fi = jnp.concatenate([f_ref[order_ref[k], 1] for k in range(len(at_refs))], axis=0)
    re_ref[0:ROW_MAX] = jnp.zeros((ROW_MAX, cols), jnp.float32)
    im_ref[0:ROW_MAX] = jnp.zeros((ROW_MAX, cols), jnp.float32)
    step = 256
    for r0 in range(0, rows, step):
        ar = jnp.concatenate([ref[0, :, r0 : r0 + step] for ref in at_refs], axis=0)
        ai = jnp.concatenate([ref[1, :, r0 : r0 + step] for ref in at_refs], axis=0)
        re_ref[ROW_MAX + r0 : ROW_MAX + r0 + step] = dot(ar, fr, 0, 0) - dot(ai, fi, 0, 0)
        im_ref[ROW_MAX + r0 : ROW_MAX + r0 + step] = dot(ar, fi, 0, 0) + dot(ai, fr, 0, 0)
    block = 128
    start = ROW_MAX - lag
    base = pl.multiple_of(start // 8 * 8, 8)
    rest = start - base

    def shifted(ref, r0):
        wide = ref[pl.ds(base + r0, block + 8)]
        return pltpu.roll(wide, block + 8 - rest, 0)[:block]

    sub = lax.broadcasted_iota(jnp.int32, (block // 8, 8, cols), 1)
    for r0 in range(0, rows, block):
        re = shifted(re_ref, r0).reshape(block // 8, 8, cols)
        im = shifted(im_ref, r0).reshape(block // 8, 8, cols)
        first = jnp.where(sub < 4, re, pltpu.roll(im, 4, 1))
        second = jnp.where(sub < 4, pltpu.roll(re, 4, 1), im)
        both = jnp.stack([first, second], axis=1).reshape(2 * block, cols)
        out_ref[2 * r0 : 2 * r0 + 2 * block] = both.astype(out_ref.dtype)


def recover_kernel(img_ref, g_ref, h_ref, out_ref, y_ref):
    i = pl.program_id(0)
    xs, parts, others, eight, cols = img_ref.shape
    passes = xs * others

    @pl.when(i == 0)
    def _():
        for x in range(xs):
            acc = img_ref[x, 0].astype(jnp.float32)
            for z in range(1, parts):
                acc = acc + img_ref[x, z].astype(jnp.float32)
            acc = acc.reshape(others * eight, cols)
            for c in range(cols // 128):
                y_ref[c, x * others * eight : (x + 1) * others * eight] = acc[:, c * 128 : c * 128 + 128]

    g = g_ref[...]
    h = h_ref[...]
    y = jnp.concatenate(
        [
            jnp.concatenate(
                [
                    y_ref.at[c][pl.ds(i, passes, stride=eight), :],
                    y_ref.at[c][pl.ds(eight // 2 + i, passes, stride=eight), :],
                ],
                axis=0,
            ).T
            for c in range(cols // 128)
        ],
        axis=0,
    )
    yb = y.astype(jnp.bfloat16)
    yt = yb.astype(jnp.float32)
    v = dot(yb, g, 1, 0)
    u = v - jnp.clip(v, -LEVEL, LEVEL)
    for _ in range(ITERS - 1):
        resid = yt - dot(u.astype(jnp.bfloat16), h, 1, 0)
        v = u + dot(resid.astype(jnp.bfloat16), g, 1, 0)
        u = v - jnp.clip(v, -LEVEL, LEVEL)
    out_ref[0, 0] = u[:, :BINS]
    out_ref[1, 0] = u[:, BINS:]


def steering(normal_spacings, source):
    chosen = jnp.sum(
        jnp.where(
            source[:, None] == jnp.arange(normal_spacings.shape[0], dtype=jnp.int32)[None, :],
            normal_spacings[None, :],
            0.0,
        ),
        axis=1,
    )
    bins = jnp.arange(BINS).astype(normal_spacings.dtype) - BINS // 2
    phases = jnp.pi * chosen[:, None] * bins[None, :]
    return jnp.cos(phases), jnp.sin(phases)


def body(echo, along, slant, vertical, lateral, survey, spacings):
    passes = vertical.shape[0]
    pulses = along.shape[2]
    rows = along.shape[1]
    cols = slant.shape[2]
    total = survey.shape[0]
    near = ("x", "c")
    every = ("x", "zh", "c", "y", "zl")
    bf = jnp.bfloat16

    nx = lax.axis_size("x")
    nz = lax.axis_size("zh")

    def turn(value, step):
        return lax.ppermute(value, "x", [(i, (i + step) % nx) for i in range(nx)])

    def swap(value):
        return lax.ppermute(value, "c", [(0, 1), (1, 0)])

    at = jnp.transpose(along, (0, 2, 1))
    held = [at] + [turn(at, s) for s in range(1, nx)]
    held = held + [swap(value) for value in held]
    focus = pl.pallas_call(
        focus_kernel,
        out_shape=jax.ShapeDtypeStruct((passes, 2, pulses, cols), bf),
        in_specs=[SMEM, VMEM, VMEM],
        out_specs=VMEM,
        name="focus",
    )(lateral, echo, slant)
    focus = lax.all_to_all(focus, near, 0, 0, tiled=True)
    x = lax.axis_index("x")
    c = lax.axis_index("c")
    steps = jnp.arange(2 * nx, dtype=jnp.int32)
    order = (x - steps % nx) % nx * 2 + (c + steps // nx) % 2
    image = pl.pallas_call(
        image_kernel,
        out_shape=jax.ShapeDtypeStruct((2 * rows, cols), bf),
        in_specs=[SMEM, SMEM] + [VMEM] * (2 * nx + 1),
        out_specs=VMEM,
        scratch_shapes=[pltpu.VMEM((rows + ROW_MAX + 8, cols), jnp.float32)] * 2,
        compiler_params=pltpu.CompilerParams(vmem_limit_bytes=40 << 20),
        name="image",
    )(order.astype(jnp.int32), vertical, *held, focus)
    image = lax.all_to_all(image, every, 0, 0, tiled=True)

    source = survey.reshape(total // passes, passes).T.reshape(total)
    cos, sin = steering(spacings, source)
    g = jnp.concatenate(
        [jnp.concatenate([cos, -sin], axis=1), jnp.concatenate([sin, cos], axis=1)], axis=0
    )
    gb = (g / total).astype(bf)
    hb = (g.T / BINS).astype(bf)
    own = 4
    image = image.reshape(nx, nz, total // nx, 2 * own, cols)
    return pl.pallas_call(
        recover_kernel,
        grid=(own,),
        out_shape=jax.ShapeDtypeStruct((2, own, cols, BINS), jnp.float32),
        in_specs=[
            pl.BlockSpec(image.shape, lambda i: (0, 0, 0, 0, 0)),
            pl.BlockSpec(gb.shape, lambda i: (0, 0)),
            pl.BlockSpec(hb.shape, lambda i: (0, 0)),
        ],
        out_specs=pl.BlockSpec((2, 1, cols, BINS), lambda i: (0, i, 0, 0)),
        scratch_shapes=[pltpu.VMEM((cols // 128, total * 2 * own, 128), jnp.float32)],
        compiler_params=pltpu.CompilerParams(vmem_limit_bytes=40 << 20),
        name="recover",
    )(image, gb, hb)


def solution(mesh):
    fine = Mesh(mesh.devices.reshape(4, 4, 2, 4, 2), ("x", "zh", "c", "y", "zl"))
    ap = ("x", "zh", "c")
    group = ("y", "zl")
    return jax.shard_map(
        body,
        mesh=fine,
        in_specs=(
            P(None, group, ap, None),
            P(None, None, ap),
            P(),
            P(group),
            P(group),
            P(),
            P(),
        ),
        out_specs=P(None, ap + group, None, None),
        check_vma=False,
    )
```

```python
import functools

import jax
import jax.numpy as jnp
from jax import lax
from jax.experimental import pallas as pl
from jax.experimental.pallas import tpu as pltpu
from jax.sharding import Mesh, PartitionSpec as P

BINS = 512
ITERS = 4
ROW_MAX = 64
LEVEL = 0.1

VMEM = pl.BlockSpec(memory_space=pltpu.VMEM)
SMEM = pl.BlockSpec(memory_space=pltpu.SMEM)


def dot(a, b, ca, cb):
    return lax.dot_general(a, b, (((ca,), (cb,)), ((), ())), preferred_element_type=jnp.float32)


def focus_kernel(lat_ref, echo_ref, kern_ref, out_ref):
    passes, _, pulses, cols = out_ref.shape
    kr = kern_ref[0]
    ki = kern_ref[1]
    er = echo_ref[0].reshape(passes * pulses, -1)
    ei = echo_ref[1].reshape(passes * pulses, -1)
    fr = dot(er, kr, 1, 0) - dot(ei, ki, 1, 0)
    fi = dot(er, ki, 1, 0) + dot(ei, kr, 1, 0)
    col = lax.broadcasted_iota(jnp.int32, (pulses, cols), 1)
    for q in range(passes):
        lag = lat_ref[q]
        keep = col >= lag
        for part, value in enumerate((fr, fi)):
            moved = pltpu.roll(value[q * pulses : (q + 1) * pulses], lag, 1)
            out_ref[q, part] = jnp.where(keep, moved, 0.0).astype(out_ref.dtype)


def image_kernel(sizes, order_ref, *refs):
    f_ref, out_ref, re_ref, im_ref = refs[-4:]
    at_refs = refs[:-4]
    _, _, _, cols = f_ref.shape
    rows = at_refs[0].shape[2]
    lag = order_ref[len(at_refs)]
    fr = jnp.concatenate([f_ref[order_ref[k], 0] for k in range(len(at_refs))], axis=0)
    fi = jnp.concatenate([f_ref[order_ref[k], 1] for k in range(len(at_refs))], axis=0)
    re_ref[0:ROW_MAX] = jnp.zeros((ROW_MAX, cols), jnp.float32)
    im_ref[0:ROW_MAX] = jnp.zeros((ROW_MAX, cols), jnp.float32)
    step = 256
    for r0 in range(0, rows, step):
        ar = jnp.concatenate([ref[0, :, r0 : r0 + step] for ref in at_refs], axis=0)
        ai = jnp.concatenate([ref[1, :, r0 : r0 + step] for ref in at_refs], axis=0)
        re_ref[ROW_MAX + r0 : ROW_MAX + r0 + step] = dot(ar, fr, 0, 0) - dot(ai, fi, 0, 0)
        im_ref[ROW_MAX + r0 : ROW_MAX + r0 + step] = dot(ar, fi, 0, 0) + dot(ai, fr, 0, 0)
    nx, nz, nc, ny, nl = sizes
    block = nl * ny * nc * 4
    start = ROW_MAX - lag
    base = pl.multiple_of(start // 8 * 8, 8)
    rest = start - base

    def shifted(ref, r0):
        wide = ref[pl.ds(base + r0, block + 8)]
        return pltpu.roll(wide, block + 8 - rest, 0)[:block].reshape(block // 8, 8, cols)

    sub = lax.broadcasted_iota(jnp.int32, (block // 8, 8, cols), 1)
    for x in range(nx):
        for z in range(nz):
            r0 = (x * nz + z) * block
            re = shifted(re_ref, r0)
            im = shifted(im_ref, r0)
            first = jnp.where(sub < 4, re, pltpu.roll(im, 4, 1))
            second = jnp.where(sub < 4, pltpu.roll(re, 4, 1), im)
            both = jnp.stack([first, second], axis=1).reshape(2 * block, cols).astype(out_ref.dtype)
            span = 8 * nl
            for c in range(nc):
                for y in range(ny):
                    at = (((y * nx + x) * nc + c) * nz + z) * span
                    piece = (c * ny + y) * span
                    out_ref[at : at + span] = both[piece : piece + span]


def recover_kernel(img_ref, g_ref, h_ref, out_ref, y_ref):
    i = pl.program_id(0)
    outer, parts, inner, eight, cols = img_ref.shape
    passes = outer * inner

    @pl.when(i == 0)
    def _():
        some = 8
        for k in range(0, outer, some):
            acc = img_ref[k : k + some, 0].astype(jnp.float32)
            for z in range(1, parts):
                acc = acc + img_ref[k : k + some, z].astype(jnp.float32)
            acc = acc.reshape(some * inner * eight, cols)
            at = k * inner * eight
            for c in range(cols // 128):
                y_ref[c, at : at + some * inner * eight] = acc[:, c * 128 : c * 128 + 128]

    g = g_ref[...]
    h = h_ref[...]
    chains = []
    for c in range(cols // 128):
        re = y_ref.at[c][pl.ds(i, passes, stride=eight), :]
        im = y_ref.at[c][pl.ds(eight // 2 + i, passes, stride=eight), :]
        y = jnp.concatenate([re, im], axis=0).T.astype(jnp.bfloat16)
        chains += [y[:64], y[64:]]
    wide = [y.astype(jnp.float32) for y in chains]

    def shrink(v):
        return v - jnp.clip(v, -LEVEL, LEVEL)

    us = [shrink(dot(y, g, 1, 0)) for y in chains]
    for _ in range(ITERS - 1):
        resids = [
            (y - dot(u.astype(jnp.bfloat16), h, 1, 0)).astype(jnp.bfloat16) for y, u in zip(wide, us)
        ]
        us = [shrink(u + dot(r, g, 1, 0)) for u, r in zip(us, resids)]
    for k, u in enumerate(us):
        out_ref[0, 0, k * 64 : k * 64 + 64] = u[:, :BINS]
        out_ref[1, 0, k * 64 : k * 64 + 64] = u[:, BINS:]


def steering(normal_spacings, source):
    chosen = jnp.sum(
        jnp.where(
            source[:, None] == jnp.arange(normal_spacings.shape[0], dtype=jnp.int32)[None, :],
            normal_spacings[None, :],
            0.0,
        ),
        axis=1,
    )
    bins = jnp.arange(BINS).astype(normal_spacings.dtype) - BINS // 2
    phases = jnp.pi * chosen[:, None] * bins[None, :]
    return jnp.cos(phases), jnp.sin(phases)


def body(echo, along, slant, vertical, lateral, survey, spacings):
    passes = vertical.shape[0]
    pulses = along.shape[2]
    rows = along.shape[1]
    cols = slant.shape[2]
    total = survey.shape[0]
    near = ("x", "c")
    every = ("y", "x", "c", "zh", "zl")
    bf = jnp.bfloat16

    nx = lax.axis_size("x")
    nz = lax.axis_size("zh")

    def turn(value, step):
        return lax.ppermute(value, "x", [(i, (i + step) % nx) for i in range(nx)])

    def swap(value):
        return lax.ppermute(value, "c", [(0, 1), (1, 0)])

    at = jnp.transpose(along, (0, 2, 1))
    held = [at] + [turn(at, s) for s in range(1, nx)]
    held = held + [swap(value) for value in held]
    focus = pl.pallas_call(
        focus_kernel,
        out_shape=jax.ShapeDtypeStruct((passes, 2, pulses, cols), bf),
        in_specs=[SMEM, VMEM, VMEM],
        out_specs=VMEM,
        name="focus",
    )(lateral, echo, slant)
    focus = lax.all_to_all(focus, near, 0, 0, tiled=True)
    x = lax.axis_index("x")
    c = lax.axis_index("c")
    steps = jnp.arange(2 * nx, dtype=jnp.int32)
    order = (x - steps % nx) % nx * 2 + (c + steps // nx) % 2
    lag = jnp.sum(jnp.where(jnp.arange(passes, dtype=jnp.int32) == x * 2 + c, vertical, 0))
    table = jnp.concatenate([order.astype(jnp.int32), lag.reshape(1)])
    sizes = tuple(lax.axis_size(name) for name in ("x", "zh", "c", "y", "zl"))
    image = pl.pallas_call(
        functools.partial(image_kernel, sizes),
        out_shape=jax.ShapeDtypeStruct((2 * rows, cols), bf),
        in_specs=[SMEM] + [VMEM] * (2 * nx + 1),
        out_specs=VMEM,
        scratch_shapes=[pltpu.VMEM((rows + ROW_MAX + 8, cols), jnp.float32)] * 2,
        compiler_params=pltpu.CompilerParams(vmem_limit_bytes=40 << 20),
        name="image",
    )(table, *held, focus)
    image = lax.all_to_all(image, every, 0, 0, tiled=True)

    nc, ny, nl = sizes[2:]
    source = survey.reshape(ny, nl, nx, nc).transpose(0, 2, 3, 1).reshape(total)
    cos, sin = steering(spacings, source)
    g = jnp.concatenate(
        [jnp.concatenate([cos, -sin], axis=1), jnp.concatenate([sin, cos], axis=1)], axis=0
    )
    gb = (g / total).astype(bf)
    hb = (g.T / BINS).astype(bf)
    own = 4
    image = image.reshape(total // nl, nz, nl, 2 * own, cols)
    return pl.pallas_call(
        recover_kernel,
        grid=(own,),
        out_shape=jax.ShapeDtypeStruct((2, own, cols, BINS), jnp.float32),
        in_specs=[
            pl.BlockSpec(image.shape, lambda i: (0, 0, 0, 0, 0)),
            pl.BlockSpec(gb.shape, lambda i: (0, 0)),
            pl.BlockSpec(hb.shape, lambda i: (0, 0)),
        ],
        out_specs=pl.BlockSpec((2, 1, cols, BINS), lambda i: (0, i, 0, 0)),
        scratch_shapes=[pltpu.VMEM((cols // 128, total * 2 * own, 128), jnp.float32)],
        compiler_params=pltpu.CompilerParams(vmem_limit_bytes=40 << 20),
        name="recover",
    )(image, gb, hb)


def solution(mesh):
    fine = Mesh(mesh.devices.reshape(4, 4, 2, 4, 2), ("x", "zh", "c", "y", "zl"))
    ap = ("x", "zh", "c")
    group = ("y", "zl")
    return jax.shard_map(
        body,
        mesh=fine,
        in_specs=(
            P(None, group, ap, None),
            P(None, None, ap),
            P(),
            P(group),
            P(group),
            P(),
            P(),
        ),
        out_specs=P(None, ap + group, None, None),
        check_vma=False,
    )
```

```python
import functools

import jax
import jax.numpy as jnp
from jax import lax
from jax.experimental import pallas as pl
from jax.experimental.pallas import tpu as pltpu
from jax.sharding import Mesh, PartitionSpec as P

BINS = 512
ITERS = 4
ROW_MAX = 64
LEVEL = 0.1

VMEM = pl.BlockSpec(memory_space=pltpu.VMEM)
SMEM = pl.BlockSpec(memory_space=pltpu.SMEM)
HBM = pl.BlockSpec(memory_space=pltpu.HBM)


def dot(a, b, ca, cb):
    return lax.dot_general(a, b, (((ca,), (cb,)), ((), ())), preferred_element_type=jnp.float32)


def focus_kernel(lat_ref, echo_ref, kern_ref, *refs):
    outs = refs[:-4]
    echo, kern, echo_sem, kern_sem = refs[-4:]
    _, _, pulses, cols = outs[0].shape
    x = lax.axis_index("x")
    c = lax.axis_index("c")
    numbers = [[(x + s) % len(outs) * 2 + (c + k) % 2 for k in range(2)] for s in range(len(outs))]

    def kern_copy(part):
        return pltpu.make_async_copy(kern_ref.at[part], kern.at[part], kern_sem.at[part])

    def echo_copy(s, k, part):
        return pltpu.make_async_copy(
            echo_ref.at[part, numbers[s][k]], echo.at[part, s, k], echo_sem.at[part, s, k]
        )

    pieces = [(s, k, part) for s in range(len(outs)) for k in range(2) for part in range(2)]
    for part in range(2):
        kern_copy(part).start()
    for piece in pieces:
        echo_copy(*piece).start()
    for part in range(2):
        kern_copy(part).wait()
    kr = kern[0]
    ki = kern[1]
    col = lax.broadcasted_iota(jnp.int32, (pulses, cols), 1)
    for s, out in enumerate(outs):
        for k in range(2):
            for part in range(2):
                echo_copy(s, k, part).wait()
        er = echo[0, s].reshape(2 * pulses, -1)
        ei = echo[1, s].reshape(2 * pulses, -1)
        fr = dot(er, kr, 1, 0) - dot(ei, ki, 1, 0)
        fi = dot(er, ki, 1, 0) + dot(ei, kr, 1, 0)
        for k in range(2):
            lag = lat_ref[numbers[s][k]]
            keep = col >= lag
            for part, value in enumerate((fr, fi)):
                moved = pltpu.roll(value[k * pulses : (k + 1) * pulses], lag, 1)
                out[k, part] = jnp.where(keep, moved, 0.0).astype(out.dtype)


def image_kernel(far, lag_ref, at_ref, own_ref, *refs):
    out_ref, at_mem, own_mem, out_mem, re_ref, im_ref, at_sem, own_sem, out_sem = refs[-9:]
    tables = list(refs[:-9])
    focus_refs = [own_mem] + tables[-2 * far + 1 :]
    held = tables[: -2 * far + 1]
    rows = at_mem.shape[2]
    cols = out_ref.shape[1]
    load_own = pltpu.make_async_copy(own_ref.at[0], own_mem.at[0], own_sem)
    load = pltpu.make_async_copy(at_ref, at_mem, at_sem)
    load_own.start()
    load.start()
    load_own.wait()
    fr = jnp.concatenate([ref[i // far, 0] for i, ref in enumerate(focus_refs)], axis=0)
    fi = jnp.concatenate([ref[i // far, 1] for i, ref in enumerate(focus_refs)], axis=0)
    re_ref[0:ROW_MAX] = jnp.zeros((ROW_MAX, cols), jnp.float32)
    im_ref[0:ROW_MAX] = jnp.zeros((ROW_MAX, cols), jnp.float32)
    lag = lag_ref[0]
    start = ROW_MAX - lag
    base = pl.multiple_of(start // 8 * 8, 8)
    rest = start - base
    step = 128
    sub = lax.broadcasted_iota(jnp.int32, (step // 8, 8, cols), 1)
    load.wait()
    def planes(refs):
        mine, one, two_r, two_i, three = refs
        return (
            [mine.at[0], one.at[0], two_r, three.at[0]],
            [mine.at[1], one.at[1], two_i, three.at[1]],
        )

    own = planes([at_mem] + held[:4])
    sibling = planes(held[4:])
    real = own[0] + sibling[0]
    imag = own[1] + sibling[1]

    def product(r0):
        ar = jnp.concatenate([ref[:, r0 : r0 + step] for ref in real], axis=0)
        ai = jnp.concatenate([ref[:, r0 : r0 + step] for ref in imag], axis=0)
        return dot(ar, fr, 0, 0) - dot(ai, fi, 0, 0), dot(ar, fi, 0, 0) + dot(ai, fr, 0, 0)

    def keep(r0, value):
        re_ref[ROW_MAX + r0 : ROW_MAX + r0 + step] = value[0]
        im_ref[ROW_MAX + r0 : ROW_MAX + r0 + step] = value[1]

    def shifted(ref, r0):
        wide = ref[pl.ds(base + r0, step + 8)]
        return pltpu.roll(wide, step + 8 - rest, 0)[:step].reshape(step // 8, 8, cols)

    def copy(r0):
        piece = pl.ds(2 * r0, 2 * step)
        return pltpu.make_async_copy(out_mem.at[piece], out_ref.at[piece], out_sem.at[r0 // step])

    keep(0, product(0))
    for r0 in range(0, rows, step):
        last = r0 + step == rows
        value = None if last else product(r0 + step)
        re = shifted(re_ref, r0)
        im = shifted(im_ref, r0)
        first = jnp.where(sub < 4, re, pltpu.roll(im, 4, 1))
        second = jnp.where(sub < 4, pltpu.roll(re, 4, 1), im)
        both = jnp.stack([first, second], axis=1).reshape(2 * step, cols)
        out_mem[2 * r0 : 2 * r0 + 2 * step] = both.astype(out_mem.dtype)
        copy(r0).start()
        if not last:
            keep(r0 + step, value)
    for r0 in range(0, rows, step):
        copy(r0).wait()


def recover_kernel(img_ref, g_ref, h_ref, out_ref, y_ref):
    i = pl.program_id(0)
    outer, parts, inner, eight, cols = img_ref.shape
    passes = outer * inner

    @pl.when(i == 0)
    def _():
        some = 1
        for k in range(0, outer, some):
            acc = img_ref[k : k + some, 0].astype(jnp.float32)
            for z in range(1, parts):
                acc = acc + img_ref[k : k + some, z].astype(jnp.float32)
            acc = acc.reshape(some * inner * eight, cols)
            at = k * inner * eight
            for c in range(cols // 128):
                y_ref[c, at : at + some * inner * eight] = acc[:, c * 128 : c * 128 + 128]

    g = g_ref[...]
    h = h_ref[...]
    chains = []
    for c in range(cols // 128):
        re = y_ref.at[c][pl.ds(i, passes, stride=eight), :]
        im = y_ref.at[c][pl.ds(eight // 2 + i, passes, stride=eight), :]
        y = jnp.concatenate([re, im], axis=0).T.astype(jnp.bfloat16)
        chains += [y[:64], y[64:]]
    wide = [y.astype(jnp.float32) for y in chains]

    def shrink(v):
        return v - jnp.clip(v, -LEVEL, LEVEL)

    us = [shrink(dot(y, g, 1, 0)) for y in chains]
    for _ in range(ITERS - 1):
        resids = [
            (y - dot(u.astype(jnp.bfloat16), h, 1, 0)).astype(jnp.bfloat16) for y, u in zip(wide, us)
        ]
        us = [shrink(u + dot(r, g, 1, 0)) for u, r in zip(us, resids)]
    for k, u in enumerate(us):
        out_ref[0, 0, k * 64 : k * 64 + 64] = u[:, :BINS]
        out_ref[1, 0, k * 64 : k * 64 + 64] = u[:, BINS:]


def steering(normal_spacings, source):
    chosen = jnp.sum(
        jnp.where(
            source[:, None] == jnp.arange(normal_spacings.shape[0], dtype=jnp.int32)[None, :],
            normal_spacings[None, :],
            0.0,
        ),
        axis=1,
    )
    bins = jnp.arange(BINS).astype(normal_spacings.dtype) - BINS // 2
    phases = jnp.pi * chosen[:, None] * bins[None, :]
    return jnp.cos(phases), jnp.sin(phases)


def partial_image(echo, along, slant, vertical, lateral):
    passes = vertical.shape[0]
    pulses = along.shape[2]
    rows = along.shape[1]
    freqs, cols = slant.shape[1:]
    bf = jnp.bfloat16
    nx = lax.axis_size("x")

    def turn(value, step):
        return lax.ppermute(value, "x", [(i, (i + step) % nx) for i in range(nx)])

    def swap(value):
        return lax.ppermute(value, "c", [(0, 1), (1, 0)])

    at = jnp.transpose(along, (0, 2, 1))
    one = turn(at, 1)
    three = turn(at, 3)
    two_re = turn(one[0], 1)
    two_im = turn(three[1], 3)

    focus = pl.pallas_call(
        focus_kernel,
        out_shape=[jax.ShapeDtypeStruct((2, 2, pulses, cols), bf)] * nx,
        in_specs=[SMEM, HBM, HBM],
        out_specs=[VMEM] * nx,
        scratch_shapes=[
            pltpu.VMEM((2, nx, 2, pulses, freqs), bf),
            pltpu.VMEM((2, freqs, cols), bf),
            pltpu.SemaphoreType.DMA((2, nx, 2)),
            pltpu.SemaphoreType.DMA((2,)),
        ],
        name="focus",
    )(lateral, echo, slant)
    focus = [focus[0]] + [turn(focus[s], s) for s in range(1, nx)]
    at_late, one_late, three_late, *focus = lax.optimization_barrier((at, one, three, *focus))
    focus = focus + [swap(value) for value in focus]
    held = [one, two_re, two_im, three]
    held = held + [swap(value) for value in (at_late, one_late, two_re, two_im, three_late)]

    number = lax.axis_index("x") * 2 + lax.axis_index("c")
    lag = jnp.sum(jnp.where(jnp.arange(passes, dtype=jnp.int32) == number, vertical, 0))
    return pl.pallas_call(
        functools.partial(image_kernel, nx),
        out_shape=jax.ShapeDtypeStruct((2 * rows, cols), bf),
        in_specs=[SMEM, HBM, HBM] + [VMEM] * (len(held) + len(focus) - 1),
        out_specs=HBM,
        scratch_shapes=[
            pltpu.VMEM((2, pulses, rows), bf),
            pltpu.VMEM((1, 2, pulses, cols), bf),
            pltpu.VMEM((2 * rows, cols), bf),
            pltpu.VMEM((rows + ROW_MAX + 8, cols), jnp.float32),
            pltpu.VMEM((rows + ROW_MAX + 8, cols), jnp.float32),
            pltpu.SemaphoreType.DMA,
            pltpu.SemaphoreType.DMA,
            pltpu.SemaphoreType.DMA((rows // 128,)),
        ],
        compiler_params=pltpu.CompilerParams(vmem_limit_bytes=40 << 20),
        name="image",
    )(lag.reshape(1), at, focus[0], *held, *focus[1:])


def body(echo, along, slant, vertical, lateral, survey, spacings):
    total = survey.shape[0]
    cols = slant.shape[2]
    bf = jnp.bfloat16
    nx, nz, nc, ny, nl = (lax.axis_size(name) for name in ("x", "zh", "c", "y", "zl"))
    image = partial_image(echo, along, slant, vertical, lateral)
    image = lax.all_to_all(image, ("x", "zh", "c", "y", "zl"), 0, 0, tiled=True)

    source = survey.reshape(ny * nl, nx * nc).T.reshape(total)
    cos, sin = steering(spacings, source)
    g = jnp.concatenate(
        [jnp.concatenate([cos, -sin], axis=1), jnp.concatenate([sin, cos], axis=1)], axis=0
    )
    gb = (g / total).astype(bf)
    hb = (g.T / BINS).astype(bf)
    own = 4
    image = image.reshape(nx, nz, nc * ny * nl, 2 * own, cols)
    return pl.pallas_call(
        recover_kernel,
        grid=(own,),
        out_shape=jax.ShapeDtypeStruct((2, own, cols, BINS), jnp.float32),
        in_specs=[
            pl.BlockSpec(image.shape, lambda i: (0, 0, 0, 0, 0)),
            pl.BlockSpec(gb.shape, lambda i: (0, 0)),
            pl.BlockSpec(hb.shape, lambda i: (0, 0)),
        ],
        out_specs=pl.BlockSpec((2, 1, cols, BINS), lambda i: (0, i, 0, 0)),
        scratch_shapes=[pltpu.VMEM((cols // 128, total * 2 * own, 128), jnp.float32)],
        compiler_params=pltpu.CompilerParams(vmem_limit_bytes=40 << 20),
        name="recover",
    )(image, gb, hb)


def solution(mesh):
    fine = Mesh(mesh.devices.reshape(4, 4, 2, 4, 2), ("x", "zh", "c", "y", "zl"))
    ap = ("x", "zh", "c")
    group = ("y", "zl")
    return jax.shard_map(
        body,
        mesh=fine,
        in_specs=(
            P(None, group, ap, None),
            P(None, None, ap),
            P(),
            P(group),
            P(group),
            P(),
            P(),
        ),
        out_specs=P(None, ap + group, None, None),
        check_vma=False,
    )
```

```python
import functools

import jax
import jax.numpy as jnp
from jax import lax
from jax.experimental import pallas as pl
from jax.experimental.pallas import tpu as pltpu
from jax.sharding import Mesh, PartitionSpec as P

BINS = 512
ITERS = 4
ROW_MAX = 64
LEVEL = 0.1

VMEM = pl.BlockSpec(memory_space=pltpu.VMEM)
SMEM = pl.BlockSpec(memory_space=pltpu.SMEM)
HBM = pl.BlockSpec(memory_space=pltpu.HBM)


def dot(a, b, ca, cb):
    return lax.dot_general(a, b, (((ca,), (cb,)), ((), ())), preferred_element_type=jnp.float32)


def focus_kernel(lat_ref, ver_ref, echo_ref, kern_ref, *outs):
    _, passes, pulses, _ = echo_ref.shape
    cols = kern_ref.shape[2]
    far = len(outs)
    x = lax.axis_index("x")
    c = lax.axis_index("c")
    pairs = [(x + s) % far * 2 for s in range(far)]
    kr = kern_ref[0]
    ki = kern_ref[1]
    er, ei = (
        jnp.concatenate(
            [echo_ref[part, pl.ds(pair, 2)].reshape(2 * pulses, -1) for pair in pairs], axis=0
        )
        for part in range(2)
    )
    fr = dot(er, kr, 1, 0) - dot(ei, ki, 1, 0)
    fi = dot(er, ki, 1, 0) + dot(ei, kr, 1, 0)
    col = lax.broadcasted_iota(jnp.int32, (pulses, cols), 1)
    for s, out in enumerate(outs):
        for p in range(2):
            lag = lat_ref[pairs[s] + p]
            keep = col >= lag
            at = (2 * s + p) * pulses
            for part, value in enumerate((fr, fi)):
                moved = pltpu.roll(value[at : at + pulses], lag, 1)
                out[(c + p) % 2, part, 0:pulses] = jnp.where(keep, moved, 0.0).astype(out.dtype)
    extra = outs[0].shape[2] - pulses
    row_lag = jnp.full((extra, cols), ver_ref[pairs[0] + c].astype(jnp.float32))
    for k in range(2):
        for part in range(2):
            outs[0][k, part, pulses : pulses + extra] = row_lag.astype(outs[0].dtype)


def image_kernel(far, *refs):
    out_ref, out_mem, re_ref, im_ref, out_sem = refs[-5:]
    tables = list(refs[:-5])
    focus_refs = tables[-2 * far :]
    held = tables[: -2 * far]
    _, pulses, rows = held[0].shape
    cols = out_ref.shape[1]
    fr = jnp.concatenate([ref[i // far, 0, 0:pulses] for i, ref in enumerate(focus_refs)], axis=0)
    fi = jnp.concatenate([ref[i // far, 1, 0:pulses] for i, ref in enumerate(focus_refs)], axis=0)
    lag = jnp.max(focus_refs[0][0, 0, pulses:].astype(jnp.float32)).astype(jnp.int32)
    re_ref[0:ROW_MAX] = jnp.zeros((ROW_MAX, cols), jnp.float32)
    im_ref[0:ROW_MAX] = jnp.zeros((ROW_MAX, cols), jnp.float32)
    start = ROW_MAX - lag
    base = pl.multiple_of(start // 8 * 8, 8)
    rest = start - base
    step = 128
    sub = lax.broadcasted_iota(jnp.int32, (step // 8, 8, cols), 1)
    def planes(refs):
        mine, one, two_r, two_i, three = refs
        return (
            [mine.at[0], one.at[0], two_r, three.at[0]],
            [mine.at[1], one.at[1], two_i, three.at[1]],
        )

    own = planes(held[:5])
    sibling = planes(held[5:])
    real = own[0] + sibling[0]
    imag = own[1] + sibling[1]

    def product(r0):
        ar = jnp.concatenate([ref[:, r0 : r0 + step] for ref in real], axis=0)
        ai = jnp.concatenate([ref[:, r0 : r0 + step] for ref in imag], axis=0)
        return dot(ar, fr, 0, 0) - dot(ai, fi, 0, 0), dot(ar, fi, 0, 0) + dot(ai, fr, 0, 0)

    def keep(r0, value):
        re_ref[ROW_MAX + r0 : ROW_MAX + r0 + step] = value[0]
        im_ref[ROW_MAX + r0 : ROW_MAX + r0 + step] = value[1]

    def shifted(ref, r0):
        wide = ref[pl.ds(base + r0, step + 8)]
        return pltpu.roll(wide, step + 8 - rest, 0)[:step].reshape(step // 8, 8, cols)

    def copy(r0):
        piece = pl.ds(2 * r0, 2 * step)
        return pltpu.make_async_copy(out_mem.at[piece], out_ref.at[piece], out_sem.at[r0 // step])

    keep(0, product(0))
    for r0 in range(0, rows, step):
        last = r0 + step == rows
        value = None if last else product(r0 + step)
        re = shifted(re_ref, r0)
        im = shifted(im_ref, r0)
        first = jnp.where(sub < 4, re, pltpu.roll(im, 4, 1))
        second = jnp.where(sub < 4, pltpu.roll(re, 4, 1), im)
        both = jnp.stack([first, second], axis=1).reshape(2 * step, cols)
        out_mem[2 * r0 : 2 * r0 + 2 * step] = both.astype(out_mem.dtype)
        copy(r0).start()
        if not last:
            keep(r0 + step, value)
    for r0 in range(0, rows, step):
        copy(r0).wait()


def recover_kernel(img_ref, g_ref, h_ref, out_ref, y_ref):
    i = pl.program_id(0)
    outer, parts, inner, eight, cols = img_ref.shape
    passes = outer * inner

    @pl.when(i == 0)
    def _():
        some = 1
        for k in range(0, outer, some):
            acc = img_ref[k : k + some, 0].astype(jnp.float32)
            for z in range(1, parts):
                acc = acc + img_ref[k : k + some, z].astype(jnp.float32)
            acc = acc.reshape(some * inner * eight, cols)
            at = k * inner * eight
            for c in range(cols // 128):
                y_ref[c, at : at + some * inner * eight] = acc[:, c * 128 : c * 128 + 128]

    g = g_ref[...]
    h = h_ref[...]
    chains = []
    for c in range(cols // 128):
        re = y_ref.at[c][pl.ds(i, passes, stride=eight), :]
        im = y_ref.at[c][pl.ds(eight // 2 + i, passes, stride=eight), :]
        y = jnp.concatenate([re, im], axis=0).T.astype(jnp.bfloat16)
        chains += [y[:64], y[64:]]
    wide = [y.astype(jnp.float32) for y in chains]

    def shrink(v):
        return v - jnp.clip(v, -LEVEL, LEVEL)

    us = [shrink(dot(y, g, 1, 0)) for y in chains]
    for _ in range(ITERS - 1):
        resids = [
            (y - dot(u.astype(jnp.bfloat16), h, 1, 0)).astype(jnp.bfloat16) for y, u in zip(wide, us)
        ]
        us = [shrink(u + dot(r, g, 1, 0)) for u, r in zip(us, resids)]
    for k, u in enumerate(us):
        out_ref[0, 0, k * 64 : k * 64 + 64] = u[:, :BINS]
        out_ref[1, 0, k * 64 : k * 64 + 64] = u[:, BINS:]


def steering(normal_spacings, source):
    chosen = jnp.sum(
        jnp.where(
            source[:, None] == jnp.arange(normal_spacings.shape[0], dtype=jnp.int32)[None, :],
            normal_spacings[None, :],
            0.0,
        ),
        axis=1,
    )
    bins = jnp.arange(BINS).astype(normal_spacings.dtype) - BINS // 2
    phases = jnp.pi * chosen[:, None] * bins[None, :]
    return jnp.cos(phases), jnp.sin(phases)


def partial_image(echo, along, slant, vertical, lateral):
    passes = vertical.shape[0]
    pulses = along.shape[2]
    rows = along.shape[1]
    freqs, cols = slant.shape[1:]
    bf = jnp.bfloat16
    nx = lax.axis_size("x")

    def turn(value, step):
        return lax.ppermute(value, "x", [(i, (i + step) % nx) for i in range(nx)])

    def swap(value):
        return lax.ppermute(value, "c", [(0, 1), (1, 0)])

    at = jnp.transpose(along, (0, 2, 1))
    one = turn(at, 1)
    three = turn(at, 3)
    two_re = turn(one[0], 1)
    two_im = turn(three[1], 3)

    spare = 16
    shapes = [(2, 2, pulses + spare, cols)] + [(2, 2, pulses, cols)] * (nx - 1)
    focus = pl.pallas_call(
        focus_kernel,
        out_shape=[jax.ShapeDtypeStruct(shape, bf) for shape in shapes],
        in_specs=[SMEM, SMEM, VMEM, VMEM],
        out_specs=[VMEM] * nx,
        name="focus",
    )(lateral, vertical, echo, slant)
    focus = [focus[0]] + [turn(focus[s], s) for s in range(1, nx)]
    at_late, one_late, three_late, *focus = lax.optimization_barrier((at, one, three, *focus))
    focus = focus + [swap(value) for value in focus]
    held = [one, two_re, two_im, three]
    swapped = [swap(value) for value in (at_late, one_late, two_re, two_im, three_late)]
    inside = lax.axis_index("x") < nx
    focus[0] = jnp.where(inside, focus[0], jnp.zeros_like(focus[0]))
    held = [jnp.where(inside, at_late, jnp.zeros_like(at))] + held + swapped
    return pl.pallas_call(
        functools.partial(image_kernel, nx),
        out_shape=jax.ShapeDtypeStruct((2 * rows, cols), bf),
        in_specs=[VMEM] * (len(held) + len(focus)),
        out_specs=HBM,
        scratch_shapes=[
            pltpu.VMEM((2 * rows, cols), bf),
            pltpu.VMEM((rows + ROW_MAX + 8, cols), jnp.float32),
            pltpu.VMEM((rows + ROW_MAX + 8, cols), jnp.float32),
            pltpu.SemaphoreType.DMA((rows // 128,)),
        ],
        compiler_params=pltpu.CompilerParams(vmem_limit_bytes=40 << 20),
        name="image",
    )(*held, *focus)


def body(echo, along, slant, vertical, lateral, survey, spacings):
    total = survey.shape[0]
    cols = slant.shape[2]
    bf = jnp.bfloat16
    nx, nz, nc, ny, nl = (lax.axis_size(name) for name in ("x", "zh", "c", "y", "zl"))
    image = partial_image(echo, along, slant, vertical, lateral)
    image = lax.all_to_all(image, ("x", "zh", "c", "y", "zl"), 0, 0, tiled=True)

    source = survey.reshape(ny * nl, nx * nc).T.reshape(total)
    cos, sin = steering(spacings, source)
    g = jnp.concatenate(
        [jnp.concatenate([cos, -sin], axis=1), jnp.concatenate([sin, cos], axis=1)], axis=0
    )
    gb = (g / total).astype(bf)
    hb = (g.T / BINS).astype(bf)
    own = 4
    image = image.reshape(nx, nz, nc * ny * nl, 2 * own, cols)
    return pl.pallas_call(
        recover_kernel,
        grid=(own,),
        out_shape=jax.ShapeDtypeStruct((2, own, cols, BINS), jnp.float32),
        in_specs=[
            pl.BlockSpec(image.shape, lambda i: (0, 0, 0, 0, 0)),
            pl.BlockSpec(gb.shape, lambda i: (0, 0)),
            pl.BlockSpec(hb.shape, lambda i: (0, 0)),
        ],
        out_specs=pl.BlockSpec((2, 1, cols, BINS), lambda i: (0, i, 0, 0)),
        scratch_shapes=[pltpu.VMEM((cols // 128, total * 2 * own, 128), jnp.float32)],
        compiler_params=pltpu.CompilerParams(vmem_limit_bytes=40 << 20),
        name="recover",
    )(image, gb, hb)


def solution(mesh):
    fine = Mesh(mesh.devices.reshape(4, 4, 2, 4, 2), ("x", "zh", "c", "y", "zl"))
    ap = ("x", "zh", "c")
    group = ("y", "zl")
    return jax.shard_map(
        body,
        mesh=fine,
        in_specs=(
            P(None, group, ap, None),
            P(None, None, ap),
            P(),
            P(group),
            P(group),
            P(),
            P(),
        ),
        out_specs=P(None, ap + group, None, None),
        check_vma=False,
    )
```

```python
import functools

import jax
import jax.numpy as jnp
from jax import lax
from jax.experimental import pallas as pl
from jax.experimental.pallas import tpu as pltpu
from jax.sharding import Mesh, PartitionSpec as P

BINS = 512
ITERS = 4
ROW_MAX = 64
LEVEL = 0.1

VMEM = pl.BlockSpec(memory_space=pltpu.VMEM)
SMEM = pl.BlockSpec(memory_space=pltpu.SMEM)
HBM = pl.BlockSpec(memory_space=pltpu.HBM)


def dot(a, b, ca, cb):
    return lax.dot_general(a, b, (((ca,), (cb,)), ((), ())), preferred_element_type=jnp.float32)


def focus_kernel(lat_ref, ver_ref, echo_ref, kern_ref, *outs):
    _, passes, pulses, _ = echo_ref.shape
    cols = kern_ref.shape[2]
    far = len(outs)
    x = lax.axis_index("x")
    c = lax.axis_index("c")
    pairs = [(x + s) % far * 2 for s in range(far)]
    kr = kern_ref[0]
    ki = kern_ref[1]
    er, ei = (
        jnp.concatenate(
            [echo_ref[part, pl.ds(pair, 2)].reshape(2 * pulses, -1) for pair in pairs], axis=0
        )
        for part in range(2)
    )
    fr = dot(er, kr, 1, 0) - dot(ei, ki, 1, 0)
    fi = dot(er, ki, 1, 0) + dot(ei, kr, 1, 0)
    col = lax.broadcasted_iota(jnp.int32, (pulses, cols), 1)
    for s, out in enumerate(outs):
        for p in range(2):
            lag = lat_ref[pairs[s] + p]
            keep = col >= lag
            at = (2 * s + p) * pulses
            for part, value in enumerate((fr, fi)):
                moved = pltpu.roll(value[at : at + pulses], lag, 1)
                out[(c + p) % 2, part, 0:pulses] = jnp.where(keep, moved, 0.0).astype(out.dtype)
    extra = outs[0].shape[2] - pulses
    row_lag = jnp.full((extra, cols), ver_ref[pairs[0] + c].astype(jnp.float32))
    for k in range(2):
        for part in range(2):
            outs[0][k, part, pulses : pulses + extra] = row_lag.astype(outs[0].dtype)


def image_kernel(far, *refs):
    out_ref, out_mem, re_ref, im_ref, out_sem = refs[-5:]
    tables = list(refs[:-5])
    focus_refs = tables[-2 * far :]
    held = tables[: -2 * far]
    _, pulses, rows = held[0].shape
    cols = out_ref.shape[1]
    fr = jnp.concatenate([ref[i // far, 0, 0:pulses] for i, ref in enumerate(focus_refs)], axis=0)
    fi = jnp.concatenate([ref[i // far, 1, 0:pulses] for i, ref in enumerate(focus_refs)], axis=0)
    lag = jnp.max(focus_refs[0][0, 0, pulses:].astype(jnp.float32)).astype(jnp.int32)
    re_ref[0:ROW_MAX] = jnp.zeros((ROW_MAX, cols), jnp.float32)
    im_ref[0:ROW_MAX] = jnp.zeros((ROW_MAX, cols), jnp.float32)
    start = ROW_MAX - lag
    base = pl.multiple_of(start // 8 * 8, 8)
    rest = start - base
    step = 128
    sub = lax.broadcasted_iota(jnp.int32, (step // 8, 8, cols), 1)
    def planes(refs):
        mine, one, two_r, two_i, three = refs
        return (
            [mine.at[0], one.at[0], two_r, three.at[0]],
            [mine.at[1], one.at[1], two_i, three.at[1]],
        )

    own = planes(held[:5])
    sibling = planes(held[5:])
    real = own[0] + sibling[0]
    imag = own[1] + sibling[1]

    def product(r0):
        ar = jnp.concatenate([ref[:, r0 : r0 + step] for ref in real], axis=0)
        ai = jnp.concatenate([ref[:, r0 : r0 + step] for ref in imag], axis=0)
        return dot(ar, fr, 0, 0) - dot(ai, fi, 0, 0), dot(ar, fi, 0, 0) + dot(ai, fr, 0, 0)

    def keep(r0, value):
        re_ref[ROW_MAX + r0 : ROW_MAX + r0 + step] = value[0]
        im_ref[ROW_MAX + r0 : ROW_MAX + r0 + step] = value[1]

    def shifted(ref, r0):
        wide = ref[pl.ds(base + r0, step + 8)]
        return pltpu.roll(wide, step + 8 - rest, 0)[:step].reshape(step // 8, 8, cols)

    def copy(r0):
        piece = pl.ds(2 * r0, 2 * step)
        return pltpu.make_async_copy(out_mem.at[piece], out_ref.at[piece], out_sem.at[r0 // step])

    keep(0, product(0))
    for r0 in range(0, rows, step):
        last = r0 + step == rows
        value = None if last else product(r0 + step)
        re = shifted(re_ref, r0)
        im = shifted(im_ref, r0)
        first = jnp.where(sub < 4, re, pltpu.roll(im, 4, 1))
        second = jnp.where(sub < 4, pltpu.roll(re, 4, 1), im)
        both = jnp.stack([first, second], axis=1).reshape(2 * step, cols)
        out_mem[2 * r0 : 2 * r0 + 2 * step] = both.astype(out_mem.dtype)
        copy(r0).start()
        if not last:
            keep(r0 + step, value)
    for r0 in range(0, rows, step):
        copy(r0).wait()


def recover_kernel(img_ref, g_ref, h_ref, out_ref, y_ref):
    i = pl.program_id(0)
    outer, parts, inner, eight, cols = img_ref.shape
    passes = outer * inner

    @pl.when(i == 0)
    def _():
        some = 1
        for k in range(0, outer, some):
            acc = img_ref[k : k + some, 0].astype(jnp.float32)
            for z in range(1, parts):
                acc = acc + img_ref[k : k + some, z].astype(jnp.float32)
            acc = acc.reshape(some * inner * eight, cols)
            at = k * inner * eight
            for c in range(cols // 128):
                y_ref[c, at : at + some * inner * eight] = acc[:, c * 128 : c * 128 + 128]

    g = g_ref[...]
    h = h_ref[...]
    chains = []
    for c in range(cols // 128):
        re = y_ref.at[c][pl.ds(i, passes, stride=eight), :]
        im = y_ref.at[c][pl.ds(eight // 2 + i, passes, stride=eight), :]
        y = jnp.concatenate([re, im], axis=0).T.astype(jnp.bfloat16)
        chains += [y[:64], y[64:]]
    wide = [y.astype(jnp.float32) for y in chains]

    def shrink(v):
        return v - jnp.clip(v, -LEVEL, LEVEL)

    us = [shrink(dot(y, g, 1, 0)) for y in chains]
    for _ in range(ITERS - 1):
        resids = [
            (y - dot(u.astype(jnp.bfloat16), h, 1, 0)).astype(jnp.bfloat16) for y, u in zip(wide, us)
        ]
        us = [shrink(u + dot(r, g, 1, 0)) for u, r in zip(us, resids)]
    for k, u in enumerate(us):
        out_ref[0, 0, k * 64 : k * 64 + 64] = u[:, :BINS]
        out_ref[1, 0, k * 64 : k * 64 + 64] = u[:, BINS:]


def steering(normal_spacings, source):
    chosen = jnp.sum(
        jnp.where(
            source[:, None] == jnp.arange(normal_spacings.shape[0], dtype=jnp.int32)[None, :],
            normal_spacings[None, :],
            0.0,
        ),
        axis=1,
    )
    bins = jnp.arange(BINS).astype(normal_spacings.dtype) - BINS // 2
    phases = jnp.pi * chosen[:, None] * bins[None, :]
    return jnp.cos(phases), jnp.sin(phases)


def partial_image(echo, along, slant, vertical, lateral):
    passes = vertical.shape[0]
    pulses = along.shape[2]
    rows = along.shape[1]
    freqs, cols = slant.shape[1:]
    bf = jnp.bfloat16
    nx = lax.axis_size("x")

    def turn(value, step):
        return lax.ppermute(value, "x", [(i, (i + step) % nx) for i in range(nx)])

    def swap(value):
        return lax.ppermute(value, "c", [(0, 1), (1, 0)])

    at = jnp.transpose(along, (0, 2, 1))
    one = turn(at, 1)
    three = turn(at, 3)
    two_re = turn(one[0], 1)
    two_im = turn(three[1], 3)

    spare = 16
    shapes = [(2, 2, pulses + spare, cols)] + [(2, 2, pulses, cols)] * (nx - 1)
    focus = pl.pallas_call(
        focus_kernel,
        out_shape=[jax.ShapeDtypeStruct(shape, bf) for shape in shapes],
        in_specs=[SMEM, SMEM, VMEM, VMEM],
        out_specs=[VMEM] * nx,
        name="focus",
    )(lateral, vertical, echo, slant)
    focus = [focus[0]] + [turn(focus[s], s) for s in range(1, nx)]
    inside = lax.axis_index("x") < nx
    own = jnp.where(inside, at, jnp.zeros_like(at))
    own_focus = jnp.where(inside, focus[0], jnp.zeros_like(focus[0]))
    at_late, one_late, three_late, own, own_focus, *focus = lax.optimization_barrier(
        (at, one, three, own, own_focus, *focus)
    )
    focus = focus + [swap(value) for value in focus]
    held = [one, two_re, two_im, three]
    swapped = [swap(value) for value in (at_late, one_late, two_re, two_im, three_late)]
    focus[0] = own_focus
    held = [own] + held + swapped
    return pl.pallas_call(
        functools.partial(image_kernel, nx),
        out_shape=jax.ShapeDtypeStruct((2 * rows, cols), bf),
        in_specs=[VMEM] * (len(held) + len(focus)),
        out_specs=HBM,
        scratch_shapes=[
            pltpu.VMEM((2 * rows, cols), bf),
            pltpu.VMEM((rows + ROW_MAX + 8, cols), jnp.float32),
            pltpu.VMEM((rows + ROW_MAX + 8, cols), jnp.float32),
            pltpu.SemaphoreType.DMA((rows // 128,)),
        ],
        compiler_params=pltpu.CompilerParams(vmem_limit_bytes=40 << 20),
        name="image",
    )(*held, *focus)


def body(echo, along, slant, vertical, lateral, survey, spacings):
    total = survey.shape[0]
    cols = slant.shape[2]
    bf = jnp.bfloat16
    nx, nz, nc, ny, nl = (lax.axis_size(name) for name in ("x", "zh", "c", "y", "zl"))
    image = partial_image(echo, along, slant, vertical, lateral)
    image = lax.all_to_all(image, ("x", "zh", "c", "y", "zl"), 0, 0, tiled=True)

    source = survey.reshape(ny * nl, nx * nc).T.reshape(total)
    cos, sin = steering(spacings, source)
    g = jnp.concatenate(
        [jnp.concatenate([cos, -sin], axis=1), jnp.concatenate([sin, cos], axis=1)], axis=0
    )
    gb = (g / total).astype(bf)
    hb = (g.T / BINS).astype(bf)
    own = 4
    image = image.reshape(nx, nz, nc * ny * nl, 2 * own, cols)
    return pl.pallas_call(
        recover_kernel,
        grid=(own,),
        out_shape=jax.ShapeDtypeStruct((2, own, cols, BINS), jnp.float32),
        in_specs=[
            pl.BlockSpec(image.shape, lambda i: (0, 0, 0, 0, 0)),
            pl.BlockSpec(gb.shape, lambda i: (0, 0)),
            pl.BlockSpec(hb.shape, lambda i: (0, 0)),
        ],
        out_specs=pl.BlockSpec((2, 1, cols, BINS), lambda i: (0, i, 0, 0)),
        scratch_shapes=[pltpu.VMEM((cols // 128, total * 2 * own, 128), jnp.float32)],
        compiler_params=pltpu.CompilerParams(vmem_limit_bytes=40 << 20),
        name="recover",
    )(image, gb, hb)


def solution(mesh):
    fine = Mesh(mesh.devices.reshape(4, 4, 2, 4, 2), ("x", "zh", "c", "y", "zl"))
    ap = ("x", "zh", "c")
    group = ("y", "zl")
    return jax.shard_map(
        body,
        mesh=fine,
        in_specs=(
            P(None, group, ap, None),
            P(None, None, ap),
            P(),
            P(group),
            P(group),
            P(),
            P(),
        ),
        out_specs=P(None, ap + group, None, None),
        check_vma=False,
    )
```

```python
import functools

import jax
import jax.numpy as jnp
from jax import lax
from jax.experimental import pallas as pl
from jax.experimental.pallas import tpu as pltpu
from jax.sharding import Mesh, PartitionSpec as P

BINS = 512
ITERS = 4
ROW_MAX = 64
LEVEL = 0.1

VMEM = pl.BlockSpec(memory_space=pltpu.VMEM)
SMEM = pl.BlockSpec(memory_space=pltpu.SMEM)
HBM = pl.BlockSpec(memory_space=pltpu.HBM)


def dot(a, b, ca, cb):
    return lax.dot_general(a, b, (((ca,), (cb,)), ((), ())), preferred_element_type=jnp.float32)


def focus_kernel(lat_ref, ver_ref, echo_ref, kern_ref, *outs):
    _, passes, pulses, _ = echo_ref.shape
    cols = kern_ref.shape[2]
    far = len(outs)
    x = lax.axis_index("x")
    c = lax.axis_index("c")
    pairs = [(x + s) % far * 2 for s in range(far)]
    kr = kern_ref[0]
    ki = kern_ref[1]
    er, ei = (
        jnp.concatenate(
            [echo_ref[part, pl.ds(pair, 2)].reshape(2 * pulses, -1) for pair in pairs], axis=0
        )
        for part in range(2)
    )
    fr = dot(er, kr, 1, 0) - dot(ei, ki, 1, 0)
    fi = dot(er, ki, 1, 0) + dot(ei, kr, 1, 0)
    col = lax.broadcasted_iota(jnp.int32, (pulses, cols), 1)
    for s, out in enumerate(outs):
        for p in range(2):
            lag = lat_ref[pairs[s] + p]
            keep = col >= lag
            at = (2 * s + p) * pulses
            for part, value in enumerate((fr, fi)):
                moved = pltpu.roll(value[at : at + pulses], lag, 1)
                out[(c + p) % 2, part, 0:pulses] = jnp.where(keep, moved, 0.0).astype(out.dtype)
    extra = outs[0].shape[2] - pulses
    row_lag = jnp.full((extra, cols), ver_ref[pairs[0] + c].astype(jnp.float32))
    for k in range(2):
        for part in range(2):
            outs[0][k, part, pulses : pulses + extra] = row_lag.astype(outs[0].dtype)


def image_kernel(far, *refs):
    out_ref, out_mem, re_ref, im_ref, out_sem = refs[-5:]
    tables = list(refs[:-5])
    focus_refs = tables[-2 * far :]
    held = tables[: -2 * far]
    _, pulses, rows = held[0].shape
    cols = out_ref.shape[1]
    fr = jnp.concatenate([ref[i // far, 0, 0:pulses] for i, ref in enumerate(focus_refs)], axis=0)
    fi = jnp.concatenate([ref[i // far, 1, 0:pulses] for i, ref in enumerate(focus_refs)], axis=0)
    lag = jnp.max(focus_refs[0][0, 0, pulses:].astype(jnp.float32)).astype(jnp.int32)
    re_ref[0:ROW_MAX] = jnp.zeros((ROW_MAX, cols), jnp.float32)
    im_ref[0:ROW_MAX] = jnp.zeros((ROW_MAX, cols), jnp.float32)
    start = ROW_MAX - lag
    base = pl.multiple_of(start // 8 * 8, 8)
    rest = start - base
    step = 128
    sub = lax.broadcasted_iota(jnp.int32, (step // 8, 8, cols), 1)
    def planes(refs):
        mine, one, two_r, two_i, three = refs
        return (
            [mine.at[0], one.at[0], two_r, three.at[0]],
            [mine.at[1], one.at[1], two_i, three.at[1]],
        )

    own = planes(held[:5])
    sibling = planes(held[5:])
    real = own[0] + sibling[0]
    imag = own[1] + sibling[1]

    def product(r0):
        ar = jnp.concatenate([ref[:, r0 : r0 + step] for ref in real], axis=0)
        ai = jnp.concatenate([ref[:, r0 : r0 + step] for ref in imag], axis=0)
        return dot(ar, fr, 0, 0) - dot(ai, fi, 0, 0), dot(ar, fi, 0, 0) + dot(ai, fr, 0, 0)

    def keep(r0, value):
        re_ref[ROW_MAX + r0 : ROW_MAX + r0 + step] = value[0]
        im_ref[ROW_MAX + r0 : ROW_MAX + r0 + step] = value[1]

    def shifted(ref, r0):
        wide = ref[pl.ds(base + r0, step + 8)]
        return pltpu.roll(wide, step + 8 - rest, 0)[:step].reshape(step // 8, 8, cols)

    def copy(r0):
        piece = pl.ds(2 * r0, 2 * step)
        return pltpu.make_async_copy(out_mem.at[piece], out_ref.at[piece], out_sem.at[r0 // step])

    keep(0, product(0))
    for r0 in range(0, rows, step):
        last = r0 + step == rows
        value = None if last else product(r0 + step)
        re = shifted(re_ref, r0)
        im = shifted(im_ref, r0)
        first = jnp.where(sub < 4, re, pltpu.roll(im, 4, 1))
        second = jnp.where(sub < 4, pltpu.roll(re, 4, 1), im)
        both = jnp.stack([first, second], axis=1).reshape(2 * step, cols)
        out_mem[2 * r0 : 2 * r0 + 2 * step] = both.astype(out_mem.dtype)
        copy(r0).start()
        if not last:
            keep(r0 + step, value)
    for r0 in range(0, rows, step):
        copy(r0).wait()


def recover_kernel(img_ref, g_ref, h_ref, out_ref, y_ref):
    i = pl.program_id(0)
    outer, parts, inner, eight, cols = img_ref.shape
    passes = outer * inner

    @pl.when(i == 0)
    def _():
        some = 1
        for k in range(0, outer, some):
            acc = img_ref[k : k + some, 0].astype(jnp.float32)
            for z in range(1, parts):
                acc = acc + img_ref[k : k + some, z].astype(jnp.float32)
            acc = acc.reshape(some * inner * eight, cols)
            at = k * inner * eight
            for c in range(cols // 128):
                y_ref[c, at : at + some * inner * eight] = acc[:, c * 128 : c * 128 + 128]

    g = g_ref[...]
    h = h_ref[...]
    chains = []
    for c in range(cols // 128):
        re = y_ref.at[c][pl.ds(i, passes, stride=eight), :]
        im = y_ref.at[c][pl.ds(eight // 2 + i, passes, stride=eight), :]
        y = jnp.concatenate([re, im], axis=0).T.astype(jnp.bfloat16)
        chains += [y[:64], y[64:]]
    wide = [y.astype(jnp.float32) for y in chains]

    def shrink(v):
        return v - jnp.clip(v, -LEVEL, LEVEL)

    us = [shrink(dot(y, g, 1, 0)) for y in chains]
    for _ in range(ITERS - 1):
        resids = [
            (y - dot(u.astype(jnp.bfloat16), h, 1, 0)).astype(jnp.bfloat16) for y, u in zip(wide, us)
        ]
        us = [shrink(u + dot(r, g, 1, 0)) for u, r in zip(us, resids)]
    for k, u in enumerate(us):
        out_ref[0, 0, k * 64 : k * 64 + 64] = u[:, :BINS]
        out_ref[1, 0, k * 64 : k * 64 + 64] = u[:, BINS:]


def steering(normal_spacings, source):
    chosen = jnp.sum(
        jnp.where(
            source[:, None] == jnp.arange(normal_spacings.shape[0], dtype=jnp.int32)[None, :],
            normal_spacings[None, :],
            0.0,
        ),
        axis=1,
    )
    bins = jnp.arange(BINS).astype(normal_spacings.dtype) - BINS // 2
    phases = jnp.pi * chosen[:, None] * bins[None, :]
    return jnp.cos(phases), jnp.sin(phases)


def partial_image(echo, along, slant, vertical, lateral):
    passes = vertical.shape[0]
    pulses = along.shape[2]
    rows = along.shape[1]
    freqs, cols = slant.shape[1:]
    bf = jnp.bfloat16
    nx = lax.axis_size("x")

    def turn(value, step):
        return lax.ppermute(value, "x", [(i, (i + step) % nx) for i in range(nx)])

    def swap(value):
        return lax.ppermute(value, "c", [(0, 1), (1, 0)])

    at = jnp.transpose(along, (0, 2, 1))
    one = turn(at, 1)
    three = turn(at, 3)
    pass_re, pass_im = one[0], three[1]
    two_re = turn(pass_re, 1)
    two_im = turn(pass_im, 3)

    spare = 16
    shapes = [(2, 2, pulses + spare, cols)] + [(2, 2, pulses, cols)] * (nx - 1)
    focus = pl.pallas_call(
        focus_kernel,
        out_shape=[jax.ShapeDtypeStruct(shape, bf) for shape in shapes],
        in_specs=[SMEM, SMEM, VMEM, VMEM],
        out_specs=[VMEM] * nx,
        name="focus",
    )(lateral, vertical, echo, slant)
    focus = [focus[0]] + [turn(focus[s], s) for s in range(1, nx)]
    inside = lax.axis_index("x") < nx
    at_here, focus_here, _, _ = lax.optimization_barrier((at, focus[0], pass_re, pass_im))
    own = jnp.where(inside, at_here, jnp.zeros_like(at))
    own_focus = jnp.where(inside, focus_here, jnp.zeros_like(focus[0]))
    at_late, one_late, three_late, own, own_focus, *focus = lax.optimization_barrier(
        (at, one, three, own, own_focus, *focus)
    )
    focus = focus + [swap(value) for value in focus]
    held = [one, two_re, two_im, three]
    swapped = [swap(value) for value in (at_late, one_late, two_re, two_im, three_late)]
    focus[0] = own_focus
    held = [own] + held + swapped
    return pl.pallas_call(
        functools.partial(image_kernel, nx),
        out_shape=jax.ShapeDtypeStruct((2 * rows, cols), bf),
        in_specs=[VMEM] * (len(held) + len(focus)),
        out_specs=HBM,
        scratch_shapes=[
            pltpu.VMEM((2 * rows, cols), bf),
            pltpu.VMEM((rows + ROW_MAX + 8, cols), jnp.float32),
            pltpu.VMEM((rows + ROW_MAX + 8, cols), jnp.float32),
            pltpu.SemaphoreType.DMA((rows // 128,)),
        ],
        compiler_params=pltpu.CompilerParams(vmem_limit_bytes=40 << 20),
        name="image",
    )(*held, *focus)


def body(echo, along, slant, vertical, lateral, survey, spacings):
    total = survey.shape[0]
    cols = slant.shape[2]
    bf = jnp.bfloat16
    nx, nz, nc, ny, nl = (lax.axis_size(name) for name in ("x", "zh", "c", "y", "zl"))
    image = partial_image(echo, along, slant, vertical, lateral)
    image = lax.all_to_all(image, ("x", "zh", "c", "y", "zl"), 0, 0, tiled=True)

    source = survey.reshape(ny * nl, nx * nc).T.reshape(total)
    cos, sin = steering(spacings, source)
    g = jnp.concatenate(
        [jnp.concatenate([cos, -sin], axis=1), jnp.concatenate([sin, cos], axis=1)], axis=0
    )
    gb = (g / total).astype(bf)
    hb = (g.T / BINS).astype(bf)
    own = 4
    image = image.reshape(nx, nz, nc * ny * nl, 2 * own, cols)
    return pl.pallas_call(
        recover_kernel,
        grid=(own,),
        out_shape=jax.ShapeDtypeStruct((2, own, cols, BINS), jnp.float32),
        in_specs=[
            pl.BlockSpec(image.shape, lambda i: (0, 0, 0, 0, 0)),
            pl.BlockSpec(gb.shape, lambda i: (0, 0)),
            pl.BlockSpec(hb.shape, lambda i: (0, 0)),
        ],
        out_specs=pl.BlockSpec((2, 1, cols, BINS), lambda i: (0, i, 0, 0)),
        scratch_shapes=[pltpu.VMEM((cols // 128, total * 2 * own, 128), jnp.float32)],
        compiler_params=pltpu.CompilerParams(vmem_limit_bytes=40 << 20),
        name="recover",
    )(image, gb, hb)


def solution(mesh):
    fine = Mesh(mesh.devices.reshape(4, 4, 2, 4, 2), ("x", "zh", "c", "y", "zl"))
    ap = ("x", "zh", "c")
    group = ("y", "zl")
    return jax.shard_map(
        body,
        mesh=fine,
        in_specs=(
            P(None, group, ap, None),
            P(None, None, ap),
            P(),
            P(group),
            P(group),
            P(),
            P(),
        ),
        out_specs=P(None, ap + group, None, None),
        check_vma=False,
    )
```

```python
import functools

import jax
import jax.numpy as jnp
from jax import lax
from jax.experimental import pallas as pl
from jax.experimental.pallas import tpu as pltpu
from jax.sharding import Mesh, PartitionSpec as P

BINS = 512
ITERS = 4
ROW_MAX = 64
LEVEL = 0.1

VMEM = pl.BlockSpec(memory_space=pltpu.VMEM)
SMEM = pl.BlockSpec(memory_space=pltpu.SMEM)
HBM = pl.BlockSpec(memory_space=pltpu.HBM)


def dot(a, b, ca, cb):
    return lax.dot_general(a, b, (((ca,), (cb,)), ((), ())), preferred_element_type=jnp.float32)


def focus_kernel(lat_ref, ver_ref, echo_ref, kern_ref, *outs):
    _, passes, pulses, _ = echo_ref.shape
    cols = kern_ref.shape[2]
    far = len(outs)
    x = lax.axis_index("x")
    c = lax.axis_index("c")
    pairs = [(x + s) % far * 2 for s in range(far)]
    kr = kern_ref[0]
    ki = kern_ref[1]
    er, ei = (
        jnp.concatenate(
            [echo_ref[part, pl.ds(pair, 2)].reshape(2 * pulses, -1) for pair in pairs], axis=0
        )
        for part in range(2)
    )
    fr = dot(er, kr, 1, 0) - dot(ei, ki, 1, 0)
    fi = dot(er, ki, 1, 0) + dot(ei, kr, 1, 0)
    col = lax.broadcasted_iota(jnp.int32, (pulses, cols), 1)
    for s, out in enumerate(outs):
        for p in range(2):
            lag = lat_ref[pairs[s] + p]
            keep = col >= lag
            at = (2 * s + p) * pulses
            for part, value in enumerate((fr, fi)):
                moved = pltpu.roll(value[at : at + pulses], lag, 1)
                out[(c + p) % 2, part, 0:pulses] = jnp.where(keep, moved, 0.0).astype(out.dtype)
    extra = outs[0].shape[2] - pulses
    row_lag = jnp.full((extra, cols), ver_ref[pairs[0] + c].astype(jnp.float32))
    for k in range(2):
        for part in range(2):
            outs[0][k, part, pulses : pulses + extra] = row_lag.astype(outs[0].dtype)


def image_kernel(far, *refs):
    out_ref, out_mem, re_ref, im_ref, out_sem = refs[-5:]
    tables = list(refs[:-5])
    focus_refs = tables[-2 * far :]
    held = tables[: -2 * far]
    _, pulses, rows = held[0].shape
    cols = out_ref.shape[1]
    fr = jnp.concatenate([ref[i // far, 0, 0:pulses] for i, ref in enumerate(focus_refs)], axis=0)
    fi = jnp.concatenate([ref[i // far, 1, 0:pulses] for i, ref in enumerate(focus_refs)], axis=0)
    lag = jnp.max(focus_refs[0][0, 0, pulses:].astype(jnp.float32)).astype(jnp.int32)
    re_ref[0:ROW_MAX] = jnp.zeros((ROW_MAX, cols), jnp.float32)
    im_ref[0:ROW_MAX] = jnp.zeros((ROW_MAX, cols), jnp.float32)
    start = ROW_MAX - lag
    base = pl.multiple_of(start // 8 * 8, 8)
    rest = start - base
    step = 128
    sub = lax.broadcasted_iota(jnp.int32, (step // 8, 8, cols), 1)
    def planes(refs):
        mine, one, two_r, two_i, three = refs
        return (
            [mine.at[0], one.at[0], two_r, three.at[0]],
            [mine.at[1], one.at[1], two_i, three.at[1]],
        )

    own = planes(held[:5])
    sibling = planes(held[5:])
    real = own[0] + sibling[0]
    imag = own[1] + sibling[1]

    def product(r0):
        ar = jnp.concatenate([ref[:, r0 : r0 + step] for ref in real], axis=0)
        ai = jnp.concatenate([ref[:, r0 : r0 + step] for ref in imag], axis=0)
        return dot(ar, fr, 0, 0) - dot(ai, fi, 0, 0), dot(ar, fi, 0, 0) + dot(ai, fr, 0, 0)

    def keep(r0, value):
        re_ref[ROW_MAX + r0 : ROW_MAX + r0 + step] = value[0]
        im_ref[ROW_MAX + r0 : ROW_MAX + r0 + step] = value[1]

    def shifted(ref, r0):
        wide = ref[pl.ds(base + r0, step + 8)]
        return pltpu.roll(wide, step + 8 - rest, 0)[:step].reshape(step // 8, 8, cols)

    def copy(r0):
        piece = pl.ds(2 * r0, 2 * step)
        return pltpu.make_async_copy(out_mem.at[piece], out_ref.at[piece], out_sem.at[r0 // step])

    keep(0, product(0))
    for r0 in range(0, rows, step):
        last = r0 + step == rows
        value = None if last else product(r0 + step)
        re = shifted(re_ref, r0)
        im = shifted(im_ref, r0)
        first = jnp.where(sub < 4, re, pltpu.roll(im, 4, 1))
        second = jnp.where(sub < 4, pltpu.roll(re, 4, 1), im)
        both = jnp.stack([first, second], axis=1).reshape(2 * step, cols)
        out_mem[2 * r0 : 2 * r0 + 2 * step] = both.astype(out_mem.dtype)
        copy(r0).start()
        if not last:
            keep(r0 + step, value)
    for r0 in range(0, rows, step):
        copy(r0).wait()


def recover_kernel(img_ref, g_ref, h_ref, out_ref, y_ref):
    i = pl.program_id(0)
    outer, parts, inner, eight, cols = img_ref.shape
    passes = outer * inner

    @pl.when(i == 0)
    def _():
        some = 1
        for k in range(0, outer, some):
            acc = img_ref[k : k + some, 0].astype(jnp.float32)
            for z in range(1, parts):
                acc = acc + img_ref[k : k + some, z].astype(jnp.float32)
            acc = acc.reshape(some * inner * eight, cols)
            at = k * inner * eight
            for c in range(cols // 128):
                y_ref[c, at : at + some * inner * eight] = acc[:, c * 128 : c * 128 + 128]

    g = g_ref[...]
    h = h_ref[...]
    chains = []
    for c in range(cols // 128):
        re = y_ref.at[c][pl.ds(i, passes, stride=eight), :]
        im = y_ref.at[c][pl.ds(eight // 2 + i, passes, stride=eight), :]
        y = jnp.concatenate([re, im], axis=0).T.astype(jnp.bfloat16)
        chains += [y[:64], y[64:]]
    wide = [y.astype(jnp.float32) for y in chains]

    def shrink(v):
        return v - jnp.clip(v, -LEVEL, LEVEL)

    us = [shrink(dot(y, g, 1, 0)) for y in chains]
    for _ in range(ITERS - 1):
        resids = [
            (y - dot(u.astype(jnp.bfloat16), h, 1, 0)).astype(jnp.bfloat16) for y, u in zip(wide, us)
        ]
        us = [shrink(u + dot(r, g, 1, 0)) for u, r in zip(us, resids)]
    for k, u in enumerate(us):
        out_ref[0, 0, k * 64 : k * 64 + 64] = u[:, :BINS]
        out_ref[1, 0, k * 64 : k * 64 + 64] = u[:, BINS:]


def steering(normal_spacings, source):
    chosen = jnp.sum(
        jnp.where(
            source[:, None] == jnp.arange(normal_spacings.shape[0], dtype=jnp.int32)[None, :],
            normal_spacings[None, :],
            0.0,
        ),
        axis=1,
    )
    bins = jnp.arange(BINS).astype(normal_spacings.dtype) - BINS // 2
    phases = jnp.pi * chosen[:, None] * bins[None, :]
    return jnp.cos(phases), jnp.sin(phases)


def partial_image(echo, along, slant, vertical, lateral):
    passes = vertical.shape[0]
    pulses = along.shape[2]
    rows = along.shape[1]
    freqs, cols = slant.shape[1:]
    bf = jnp.bfloat16
    nx = lax.axis_size("x")

    def turn(value, step):
        return lax.ppermute(value, "x", [(i, (i + step) % nx) for i in range(nx)])

    def swap(value):
        return lax.ppermute(value, "c", [(0, 1), (1, 0)])

    spare = 16
    shapes = [(2, 2, pulses + spare, cols)] + [(2, 2, pulses, cols)] * (nx - 1)
    focus = pl.pallas_call(
        focus_kernel,
        out_shape=[jax.ShapeDtypeStruct(shape, bf) for shape in shapes],
        in_specs=[SMEM, SMEM, VMEM, VMEM],
        out_specs=[VMEM] * nx,
        name="focus",
    )(lateral, vertical, echo, slant)
    at, _ = lax.optimization_barrier((jnp.transpose(along, (0, 2, 1)), focus[0]))
    one = turn(at, 1)
    three = turn(at, 3)
    pass_re, pass_im = one[0], three[1]
    two_re = turn(pass_re, 1)
    two_im = turn(pass_im, 3)
    focus = [focus[0]] + [turn(focus[s], s) for s in range(1, nx)]
    inside = lax.axis_index("x") < nx
    at_here, focus_here, _, _ = lax.optimization_barrier((at, focus[0], pass_re, pass_im))
    own = jnp.where(inside, at_here, jnp.zeros_like(at))
    own_focus = jnp.where(inside, focus_here, jnp.zeros_like(focus[0]))
    at_late, one_late, three_late, own, own_focus, *focus = lax.optimization_barrier(
        (at, one, three, own, own_focus, *focus)
    )
    focus = focus + [swap(value) for value in focus]
    held = [one, two_re, two_im, three]
    swapped = [swap(value) for value in (at_late, one_late, two_re, two_im, three_late)]
    focus[0] = own_focus
    held = [own] + held + swapped
    return pl.pallas_call(
        functools.partial(image_kernel, nx),
        out_shape=jax.ShapeDtypeStruct((2 * rows, cols), bf),
        in_specs=[VMEM] * (len(held) + len(focus)),
        out_specs=HBM,
        scratch_shapes=[
            pltpu.VMEM((2 * rows, cols), bf),
            pltpu.VMEM((rows + ROW_MAX + 8, cols), jnp.float32),
            pltpu.VMEM((rows + ROW_MAX + 8, cols), jnp.float32),
            pltpu.SemaphoreType.DMA((rows // 128,)),
        ],
        compiler_params=pltpu.CompilerParams(vmem_limit_bytes=40 << 20),
        name="image",
    )(*held, *focus)


def body(echo, along, slant, vertical, lateral, survey, spacings):
    total = survey.shape[0]
    cols = slant.shape[2]
    bf = jnp.bfloat16
    nx, nz, nc, ny, nl = (lax.axis_size(name) for name in ("x", "zh", "c", "y", "zl"))
    image = partial_image(echo, along, slant, vertical, lateral)
    image = lax.all_to_all(image, ("x", "zh", "c", "y", "zl"), 0, 0, tiled=True)

    source = survey.reshape(ny * nl, nx * nc).T.reshape(total)
    cos, sin = steering(spacings, source)
    g = jnp.concatenate(
        [jnp.concatenate([cos, -sin], axis=1), jnp.concatenate([sin, cos], axis=1)], axis=0
    )
    gb = (g / total).astype(bf)
    hb = (g.T / BINS).astype(bf)
    own = 4
    image = image.reshape(nx, nz, nc * ny * nl, 2 * own, cols)
    return pl.pallas_call(
        recover_kernel,
        grid=(own,),
        out_shape=jax.ShapeDtypeStruct((2, own, cols, BINS), jnp.float32),
        in_specs=[
            pl.BlockSpec(image.shape, lambda i: (0, 0, 0, 0, 0)),
            pl.BlockSpec(gb.shape, lambda i: (0, 0)),
            pl.BlockSpec(hb.shape, lambda i: (0, 0)),
        ],
        out_specs=pl.BlockSpec((2, 1, cols, BINS), lambda i: (0, i, 0, 0)),
        scratch_shapes=[pltpu.VMEM((cols // 128, total * 2 * own, 128), jnp.float32)],
        compiler_params=pltpu.CompilerParams(vmem_limit_bytes=40 << 20),
        name="recover",
    )(image, gb, hb)


def solution(mesh):
    fine = Mesh(mesh.devices.reshape(4, 4, 2, 4, 2), ("x", "zh", "c", "y", "zl"))
    ap = ("x", "zh", "c")
    group = ("y", "zl")
    return jax.shard_map(
        body,
        mesh=fine,
        in_specs=(
            P(None, group, ap, None),
            P(None, None, ap),
            P(),
            P(group),
            P(group),
            P(),
            P(),
        ),
        out_specs=P(None, ap + group, None, None),
        check_vma=False,
    )
```

```python
import functools

import jax
import jax.numpy as jnp
from jax import lax
from jax.experimental import pallas as pl
from jax.experimental.pallas import tpu as pltpu
from jax.sharding import Mesh, PartitionSpec as P

BINS = 512
ITERS = 4
ROW_MAX = 64
LEVEL = 0.1

VMEM = pl.BlockSpec(memory_space=pltpu.VMEM)
SMEM = pl.BlockSpec(memory_space=pltpu.SMEM)
HBM = pl.BlockSpec(memory_space=pltpu.HBM)


def dot(a, b, ca, cb):
    return lax.dot_general(a, b, (((ca,), (cb,)), ((), ())), preferred_element_type=jnp.float32)


def focus_kernel(lat_ref, ver_ref, echo_ref, kern_ref, *outs):
    _, passes, pulses, _ = echo_ref.shape
    cols = kern_ref.shape[2]
    far = len(outs)
    x = lax.axis_index("x")
    c = lax.axis_index("c")
    pairs = [(x + s) % far * 2 for s in range(far)]
    kr = kern_ref[0]
    ki = kern_ref[1]
    er, ei = (
        jnp.concatenate(
            [echo_ref[part, pl.ds(pair, 2)].reshape(2 * pulses, -1) for pair in pairs], axis=0
        )
        for part in range(2)
    )
    fr = dot(er, kr, 1, 0) - dot(ei, ki, 1, 0)
    fi = dot(er, ki, 1, 0) + dot(ei, kr, 1, 0)
    col = lax.broadcasted_iota(jnp.int32, (pulses, cols), 1)
    for s, out in enumerate(outs):
        for p in range(2):
            lag = lat_ref[pairs[s] + p]
            keep = col >= lag
            at = (2 * s + p) * pulses
            for part, value in enumerate((fr, fi)):
                moved = pltpu.roll(value[at : at + pulses], lag, 1)
                out[(c + p) % 2, part, 0:pulses] = jnp.where(keep, moved, 0.0).astype(out.dtype)
    extra = outs[0].shape[2] - pulses
    row_lag = jnp.full((extra, cols), ver_ref[pairs[0] + c].astype(jnp.float32))
    for k in range(2):
        for part in range(2):
            outs[0][k, part, pulses : pulses + extra] = row_lag.astype(outs[0].dtype)


def image_kernel(far, *refs):
    out_ref, out_mem, re_ref, im_ref, out_sem = refs[-5:]
    tables = list(refs[:-5])
    focus_refs = tables[-2 * far :]
    held = tables[: -2 * far]
    _, pulses, rows = held[0].shape
    cols = out_ref.shape[1]
    fr = jnp.concatenate([ref[i // far, 0, 0:pulses] for i, ref in enumerate(focus_refs)], axis=0)
    fi = jnp.concatenate([ref[i // far, 1, 0:pulses] for i, ref in enumerate(focus_refs)], axis=0)
    lag = jnp.max(focus_refs[0][0, 0, pulses:].astype(jnp.float32)).astype(jnp.int32)
    re_ref[0:ROW_MAX] = jnp.zeros((ROW_MAX, cols), jnp.float32)
    im_ref[0:ROW_MAX] = jnp.zeros((ROW_MAX, cols), jnp.float32)
    start = ROW_MAX - lag
    base = pl.multiple_of(start // 8 * 8, 8)
    rest = start - base
    step = 128
    sub = lax.broadcasted_iota(jnp.int32, (step // 8, 8, cols), 1)
    def planes(refs):
        mine, one, two_r, two_i, three = refs
        return (
            [mine.at[0], one.at[0], two_r, three.at[0]],
            [mine.at[1], one.at[1], two_i, three.at[1]],
        )

    own = planes(held[:5])
    sibling = planes(held[5:])
    real = own[0] + sibling[0]
    imag = own[1] + sibling[1]

    def product(r0):
        ar = jnp.concatenate([ref[:, r0 : r0 + step] for ref in real], axis=0)
        ai = jnp.concatenate([ref[:, r0 : r0 + step] for ref in imag], axis=0)
        return dot(ar, fr, 0, 0) - dot(ai, fi, 0, 0), dot(ar, fi, 0, 0) + dot(ai, fr, 0, 0)

    def keep(r0, value):
        re_ref[ROW_MAX + r0 : ROW_MAX + r0 + step] = value[0]
        im_ref[ROW_MAX + r0 : ROW_MAX + r0 + step] = value[1]

    def shifted(ref, r0):
        wide = ref[pl.ds(base + r0, step + 8)]
        return pltpu.roll(wide, step + 8 - rest, 0)[:step].reshape(step // 8, 8, cols)

    def copy(r0):
        piece = pl.ds(2 * r0, 2 * step)
        return pltpu.make_async_copy(out_mem.at[piece], out_ref.at[piece], out_sem.at[r0 // step])

    keep(0, product(0))
    for r0 in range(0, rows, step):
        last = r0 + step == rows
        value = None if last else product(r0 + step)
        re = shifted(re_ref, r0)
        im = shifted(im_ref, r0)
        first = jnp.where(sub < 4, re, pltpu.roll(im, 4, 1))
        second = jnp.where(sub < 4, pltpu.roll(re, 4, 1), im)
        both = jnp.stack([first, second], axis=1).reshape(2 * step, cols)
        out_mem[2 * r0 : 2 * r0 + 2 * step] = both.astype(out_mem.dtype)
        copy(r0).start()
        if not last:
            keep(r0 + step, value)
    for r0 in range(0, rows, step):
        copy(r0).wait()


def recover_kernel(img_ref, g_ref, h_ref, out_ref, y_ref):
    i = pl.program_id(0)
    outer, parts, inner, eight, cols = img_ref.shape
    passes = outer * inner

    @pl.when(i == 0)
    def _():
        some = 1
        for k in range(0, outer, some):
            acc = img_ref[k : k + some, 0].astype(jnp.float32)
            for z in range(1, parts):
                acc = acc + img_ref[k : k + some, z].astype(jnp.float32)
            acc = acc.reshape(some * inner * eight, cols)
            at = k * inner * eight
            for c in range(cols // 128):
                y_ref[c, at : at + some * inner * eight] = acc[:, c * 128 : c * 128 + 128]

    g = g_ref[...]
    h = h_ref[...]
    chains = []
    for c in range(cols // 128):
        re = y_ref.at[c][pl.ds(i, passes, stride=eight), :]
        im = y_ref.at[c][pl.ds(eight // 2 + i, passes, stride=eight), :]
        y = jnp.concatenate([re, im], axis=0).T.astype(jnp.bfloat16)
        chains += [y[:64], y[64:]]
    wide = [y.astype(jnp.float32) for y in chains]

    def shrink(v):
        return v - jnp.clip(v, -LEVEL, LEVEL)

    us = [shrink(dot(y, g, 1, 0)) for y in chains]
    for _ in range(ITERS - 1):
        resids = [
            (y - dot(u.astype(jnp.bfloat16), h, 1, 0)).astype(jnp.bfloat16) for y, u in zip(wide, us)
        ]
        us = [shrink(u + dot(r, g, 1, 0)) for u, r in zip(us, resids)]
    for k, u in enumerate(us):
        out_ref[0, 0, k * 64 : k * 64 + 64] = u[:, :BINS]
        out_ref[1, 0, k * 64 : k * 64 + 64] = u[:, BINS:]


def steering(normal_spacings, source):
    chosen = jnp.sum(
        jnp.where(
            source[:, None] == jnp.arange(normal_spacings.shape[0], dtype=jnp.int32)[None, :],
            normal_spacings[None, :],
            0.0,
        ),
        axis=1,
    )
    bins = jnp.arange(BINS).astype(normal_spacings.dtype) - BINS // 2
    phases = jnp.pi * chosen[:, None] * bins[None, :]
    return jnp.cos(phases), jnp.sin(phases)


def partial_image(echo, along, slant, vertical, lateral):
    passes = vertical.shape[0]
    pulses = along.shape[2]
    rows = along.shape[1]
    freqs, cols = slant.shape[1:]
    bf = jnp.bfloat16
    nx = lax.axis_size("x")

    def turn(value, step):
        return lax.ppermute(value, "x", [(i, (i + step) % nx) for i in range(nx)])

    def swap(value):
        return lax.ppermute(value, "c", [(0, 1), (1, 0)])

    at = jnp.transpose(along, (0, 2, 1))
    one = turn(at, 1)
    three = turn(at, 3)
    pass_re, pass_im = one[0], three[1]
    two_re = turn(pass_re, 1)
    two_im = turn(pass_im, 3)

    spare = 16
    shapes = [(2, 2, pulses + spare, cols)] + [(2, 2, pulses, cols)] * (nx - 1)
    focus = pl.pallas_call(
        focus_kernel,
        out_shape=[jax.ShapeDtypeStruct(shape, bf) for shape in shapes],
        in_specs=[SMEM, SMEM, VMEM, VMEM],
        out_specs=[VMEM] * nx,
        name="focus",
    )(lateral, vertical, echo, slant)
    focus = [focus[0]] + [turn(focus[s], s) for s in range(1, nx)]
    inside = lax.axis_index("x") < nx
    at_here, focus_here, _, _ = lax.optimization_barrier((at, focus[0], pass_re, pass_im))
    own = jnp.where(inside, at_here, jnp.zeros_like(at))
    own_focus = jnp.where(inside, focus_here, jnp.zeros_like(focus[0]))
    at_late, one_late, three_late, own, own_focus, *focus = lax.optimization_barrier(
        (at, one, three, own, own_focus, *focus)
    )
    focus = focus + [swap(value) for value in focus]
    held = [one, two_re, two_im, three]
    swapped = [swap(value) for value in (at_late, one_late, two_re, two_im, three_late)]
    focus[0] = own_focus
    held = [own] + held + swapped
    return pl.pallas_call(
        functools.partial(image_kernel, nx),
        out_shape=jax.ShapeDtypeStruct((2 * rows, cols), bf),
        in_specs=[VMEM] * (len(held) + len(focus)),
        out_specs=HBM,
        scratch_shapes=[
            pltpu.VMEM((2 * rows, cols), bf),
            pltpu.VMEM((rows + ROW_MAX + 8, cols), jnp.float32),
            pltpu.VMEM((rows + ROW_MAX + 8, cols), jnp.float32),
            pltpu.SemaphoreType.DMA((rows // 128,)),
        ],
        compiler_params=pltpu.CompilerParams(vmem_limit_bytes=40 << 20),
        name="image",
    )(*held, *focus)


def body(echo, along, slant, vertical, lateral, survey, spacings):
    total = survey.shape[0]
    cols = slant.shape[2]
    bf = jnp.bfloat16
    nx, nz, nc, ny, nl = (lax.axis_size(name) for name in ("x", "zh", "c", "y", "zl"))
    image = partial_image(echo, along, slant, vertical, lateral)
    image = lax.all_to_all(image, ("x", "zh", "c", "y", "zl"), 0, 0, tiled=True)

    source = survey.reshape(ny * nl, nx * nc).T.reshape(total)
    cos, sin = steering(spacings, source)
    g = jnp.concatenate(
        [jnp.concatenate([cos, -sin], axis=1), jnp.concatenate([sin, cos], axis=1)], axis=0
    )
    gb = (g / total).astype(bf)
    hb = (g.T / BINS).astype(bf)
    own = 4
    image = image.reshape(nx, nz, nc * ny * nl, 2 * own, cols)
    return pl.pallas_call(
        recover_kernel,
        grid=(own,),
        out_shape=jax.ShapeDtypeStruct((2, own, cols, BINS), jnp.float32),
        in_specs=[VMEM] * 3,
        out_specs=pl.BlockSpec((2, 1, cols, BINS), lambda i: (0, i, 0, 0)),
        scratch_shapes=[pltpu.VMEM((cols // 128, total * 2 * own, 128), jnp.float32)],
        compiler_params=pltpu.CompilerParams(vmem_limit_bytes=40 << 20),
        name="recover",
    )(image, gb, hb)


def solution(mesh):
    fine = Mesh(mesh.devices.reshape(4, 4, 2, 4, 2), ("x", "zh", "c", "y", "zl"))
    ap = ("x", "zh", "c")
    group = ("y", "zl")
    return jax.shard_map(
        body,
        mesh=fine,
        in_specs=(
            P(None, group, ap, None),
            P(None, None, ap),
            P(),
            P(group),
            P(group),
            P(),
            P(),
        ),
        out_specs=P(None, ap + group, None, None),
        check_vma=False,
    )
```

```python
import functools

import jax
import jax.numpy as jnp
from jax import lax
from jax.experimental import pallas as pl
from jax.experimental.pallas import tpu as pltpu
from jax.sharding import Mesh, PartitionSpec as P

BINS = 512
ITERS = 4
ROW_MAX = 64
LEVEL = 0.1

VMEM = pl.BlockSpec(memory_space=pltpu.VMEM)
SMEM = pl.BlockSpec(memory_space=pltpu.SMEM)
HBM = pl.BlockSpec(memory_space=pltpu.HBM)


def dot(a, b, ca, cb):
    return lax.dot_general(a, b, (((ca,), (cb,)), ((), ())), preferred_element_type=jnp.float32)


def focus_kernel(lat_ref, ver_ref, echo_ref, kern_ref, *outs):
    _, passes, pulses, _ = echo_ref.shape
    cols = kern_ref.shape[2]
    far = len(outs)
    x = lax.axis_index("x")
    c = lax.axis_index("c")
    pairs = [(x + s) % far * 2 for s in range(far)]
    kr = kern_ref[0]
    ki = kern_ref[1]
    er, ei = (
        jnp.concatenate(
            [echo_ref[part, pl.ds(pair, 2)].reshape(2 * pulses, -1) for pair in pairs], axis=0
        )
        for part in range(2)
    )
    fr = dot(er, kr, 1, 0) - dot(ei, ki, 1, 0)
    fi = dot(er, ki, 1, 0) + dot(ei, kr, 1, 0)
    col = lax.broadcasted_iota(jnp.int32, (pulses, cols), 1)
    for s, out in enumerate(outs):
        for p in range(2):
            lag = lat_ref[pairs[s] + p]
            keep = col >= lag
            at = (2 * s + p) * pulses
            for part, value in enumerate((fr, fi)):
                moved = pltpu.roll(value[at : at + pulses], lag, 1)
                out[(c + p) % 2, part, 0:pulses] = jnp.where(keep, moved, 0.0).astype(out.dtype)
    extra = outs[0].shape[2] - pulses
    row_lag = jnp.full((extra, cols), ver_ref[pairs[0] + c].astype(jnp.float32))
    for k in range(2):
        for part in range(2):
            outs[0][k, part, pulses : pulses + extra] = row_lag.astype(outs[0].dtype)


def image_kernel(far, *refs):
    out_ref, out_mem, re_ref, im_ref, out_sem = refs[-5:]
    tables = list(refs[:-5])
    focus_refs = tables[-2 * far :]
    held = tables[: -2 * far]
    _, pulses, rows = held[0].shape
    cols = out_ref.shape[1]
    fr = jnp.concatenate([ref[i // far, 0, 0:pulses] for i, ref in enumerate(focus_refs)], axis=0)
    fi = jnp.concatenate([ref[i // far, 1, 0:pulses] for i, ref in enumerate(focus_refs)], axis=0)
    lag = jnp.max(focus_refs[0][0, 0, pulses:].astype(jnp.float32)).astype(jnp.int32)
    re_ref[0:ROW_MAX] = jnp.zeros((ROW_MAX, cols), jnp.float32)
    im_ref[0:ROW_MAX] = jnp.zeros((ROW_MAX, cols), jnp.float32)
    start = ROW_MAX - lag
    base = pl.multiple_of(start // 8 * 8, 8)
    rest = start - base
    step = 128
    sub = lax.broadcasted_iota(jnp.int32, (step // 8, 8, cols), 1)
    def planes(refs):
        mine, one, two_r, two_i, three = refs
        return (
            [mine.at[0], one.at[0], two_r, three.at[0]],
            [mine.at[1], one.at[1], two_i, three.at[1]],
        )

    own = planes(held[:5])
    sibling = planes(held[5:])
    real = own[0] + sibling[0]
    imag = own[1] + sibling[1]

    def product(r0):
        ar = jnp.concatenate([ref[:, r0 : r0 + step] for ref in real], axis=0)
        ai = jnp.concatenate([ref[:, r0 : r0 + step] for ref in imag], axis=0)
        return dot(ar, fr, 0, 0) - dot(ai, fi, 0, 0), dot(ar, fi, 0, 0) + dot(ai, fr, 0, 0)

    def keep(r0, value):
        re_ref[ROW_MAX + r0 : ROW_MAX + r0 + step] = value[0]
        im_ref[ROW_MAX + r0 : ROW_MAX + r0 + step] = value[1]

    def shifted(ref, r0):
        wide = ref[pl.ds(base + r0, step + 8)]
        return pltpu.roll(wide, step + 8 - rest, 0)[:step].reshape(step // 8, 8, cols)

    def copy(r0):
        piece = pl.ds(2 * r0, 2 * step)
        return pltpu.make_async_copy(out_mem.at[piece], out_ref.at[piece], out_sem.at[r0 // step])

    keep(0, product(0))
    for r0 in range(0, rows, step):
        last = r0 + step == rows
        value = None if last else product(r0 + step)
        re = shifted(re_ref, r0)
        im = shifted(im_ref, r0)
        first = jnp.where(sub < 4, re, pltpu.roll(im, 4, 1))
        second = jnp.where(sub < 4, pltpu.roll(re, 4, 1), im)
        both = jnp.stack([first, second], axis=1).reshape(2 * step, cols)
        out_mem[2 * r0 : 2 * r0 + 2 * step] = both.astype(out_mem.dtype)
        copy(r0).start()
        if not last:
            keep(r0 + step, value)
    for r0 in range(0, rows, step):
        copy(r0).wait()


def recover_kernel(img_ref, g_ref, h_ref, out_ref, y_ref):
    i = pl.program_id(0)
    outer, parts, inner, eight, cols = img_ref.shape
    passes = outer * inner

    @pl.when(i == 0)
    def _():
        some = 1
        for k in range(0, outer, some):
            acc = img_ref[k : k + some, 0].astype(jnp.float32)
            for z in range(1, parts):
                acc = acc + img_ref[k : k + some, z].astype(jnp.float32)
            acc = acc.reshape(some * inner * eight, cols)
            at = k * inner * eight
            for c in range(cols // 128):
                y_ref[c, at : at + some * inner * eight] = acc[:, c * 128 : c * 128 + 128]

    g = g_ref[...]
    h = h_ref[...]
    chains = []
    for c in range(cols // 128):
        re = y_ref.at[c][pl.ds(i, passes, stride=eight), :]
        im = y_ref.at[c][pl.ds(eight // 2 + i, passes, stride=eight), :]
        y = jnp.concatenate([re, im], axis=0).T.astype(jnp.bfloat16)
        chains += [y[:64], y[64:]]
    wide = [y.astype(jnp.float32) for y in chains]

    def shrink(v):
        return v - jnp.clip(v, -LEVEL, LEVEL)

    us = [shrink(dot(y, g, 1, 0)) for y in chains]
    for _ in range(ITERS - 1):
        resids = [
            (y - dot(u.astype(jnp.bfloat16), h, 1, 0)).astype(jnp.bfloat16) for y, u in zip(wide, us)
        ]
        us = [shrink(u + dot(r, g, 1, 0)) for u, r in zip(us, resids)]
    for k, u in enumerate(us):
        out_ref[0, 0, k * 64 : k * 64 + 64] = u[:, :BINS]
        out_ref[1, 0, k * 64 : k * 64 + 64] = u[:, BINS:]


def steering(normal_spacings, source):
    chosen = jnp.sum(
        jnp.where(
            source[:, None] == jnp.arange(normal_spacings.shape[0], dtype=jnp.int32)[None, :],
            normal_spacings[None, :],
            0.0,
        ),
        axis=1,
    )
    bins = jnp.arange(BINS).astype(normal_spacings.dtype) - BINS // 2
    phases = jnp.pi * chosen[:, None] * bins[None, :]
    return jnp.cos(phases), jnp.sin(phases)


def partial_image(echo, along, slant, vertical, lateral):
    passes = vertical.shape[0]
    pulses = along.shape[2]
    rows = along.shape[1]
    freqs, cols = slant.shape[1:]
    bf = jnp.bfloat16
    nx = lax.axis_size("x")

    def turn(value, step):
        return lax.ppermute(value, "x", [(i, (i + step) % nx) for i in range(nx)])

    def swap(value):
        return lax.ppermute(value, "c", [(0, 1), (1, 0)])

    at = jnp.transpose(along, (0, 2, 1))
    one = turn(at, 1)
    three = turn(at, 3)
    pass_re, pass_im = one[0], three[1]
    two_re = turn(pass_re, 1)
    two_im = turn(pass_im, 3)

    spare = 16
    shapes = [(2, 2, pulses + spare, cols)] + [(2, 2, pulses, cols)] * (nx - 1)
    focus = pl.pallas_call(
        focus_kernel,
        out_shape=[jax.ShapeDtypeStruct(shape, bf) for shape in shapes],
        in_specs=[SMEM, SMEM, VMEM, VMEM],
        out_specs=[VMEM] * nx,
        name="focus",
    )(lateral, vertical, echo, slant)
    moved = {s: turn(focus[s], s) for s in (1, nx - 1)}
    far_piece, _ = lax.optimization_barrier((focus[2], pass_re))
    moved[2] = turn(far_piece, 2)
    focus = [focus[0]] + [moved[s] for s in range(1, nx)]
    inside = lax.axis_index("x") < nx
    at_here, focus_here, _, _ = lax.optimization_barrier((at, focus[0], pass_re, pass_im))
    own = jnp.where(inside, at_here, jnp.zeros_like(at))
    own_focus = jnp.where(inside, focus_here, jnp.zeros_like(focus[0]))
    at_late, one_late, three_late, own, own_focus, *focus = lax.optimization_barrier(
        (at, one, three, own, own_focus, *focus)
    )
    focus = focus + [swap(value) for value in focus]
    held = [one, two_re, two_im, three]
    swapped = [swap(value) for value in (at_late, one_late, two_re, two_im, three_late)]
    focus[0] = own_focus
    held = [own] + held + swapped
    return pl.pallas_call(
        functools.partial(image_kernel, nx),
        out_shape=jax.ShapeDtypeStruct((2 * rows, cols), bf),
        in_specs=[VMEM] * (len(held) + len(focus)),
        out_specs=HBM,
        scratch_shapes=[
            pltpu.VMEM((2 * rows, cols), bf),
            pltpu.VMEM((rows + ROW_MAX + 8, cols), jnp.float32),
            pltpu.VMEM((rows + ROW_MAX + 8, cols), jnp.float32),
            pltpu.SemaphoreType.DMA((rows // 128,)),
        ],
        compiler_params=pltpu.CompilerParams(vmem_limit_bytes=40 << 20),
        name="image",
    )(*held, *focus)


def body(echo, along, slant, vertical, lateral, survey, spacings):
    total = survey.shape[0]
    cols = slant.shape[2]
    bf = jnp.bfloat16
    nx, nz, nc, ny, nl = (lax.axis_size(name) for name in ("x", "zh", "c", "y", "zl"))
    image = partial_image(echo, along, slant, vertical, lateral)
    image = lax.all_to_all(image, ("x", "zh", "c", "y", "zl"), 0, 0, tiled=True)

    source = survey.reshape(ny * nl, nx * nc).T.reshape(total)
    cos, sin = steering(spacings, source)
    g = jnp.concatenate(
        [jnp.concatenate([cos, -sin], axis=1), jnp.concatenate([sin, cos], axis=1)], axis=0
    )
    gb = (g / total).astype(bf)
    hb = (g.T / BINS).astype(bf)
    own = 4
    image = image.reshape(nx, nz, nc * ny * nl, 2 * own, cols)
    return pl.pallas_call(
        recover_kernel,
        grid=(own,),
        out_shape=jax.ShapeDtypeStruct((2, own, cols, BINS), jnp.float32),
        in_specs=[
            pl.BlockSpec(image.shape, lambda i: (0, 0, 0, 0, 0)),
            pl.BlockSpec(gb.shape, lambda i: (0, 0)),
            pl.BlockSpec(hb.shape, lambda i: (0, 0)),
        ],
        out_specs=pl.BlockSpec((2, 1, cols, BINS), lambda i: (0, i, 0, 0)),
        scratch_shapes=[pltpu.VMEM((cols // 128, total * 2 * own, 128), jnp.float32)],
        compiler_params=pltpu.CompilerParams(vmem_limit_bytes=40 << 20),
        name="recover",
    )(image, gb, hb)


def solution(mesh):
    fine = Mesh(mesh.devices.reshape(4, 4, 2, 4, 2), ("x", "zh", "c", "y", "zl"))
    ap = ("x", "zh", "c")
    group = ("y", "zl")
    return jax.shard_map(
        body,
        mesh=fine,
        in_specs=(
            P(None, group, ap, None),
            P(None, None, ap),
            P(),
            P(group),
            P(group),
            P(),
            P(),
        ),
        out_specs=P(None, ap + group, None, None),
        check_vma=False,
    )
```

```python
import functools

import jax
import jax.numpy as jnp
from jax import lax
from jax.experimental import pallas as pl
from jax.experimental.pallas import tpu as pltpu
from jax.sharding import Mesh, PartitionSpec as P

BINS = 512
ITERS = 4
ROW_MAX = 64
LEVEL = 0.1

VMEM = pl.BlockSpec(memory_space=pltpu.VMEM)
SMEM = pl.BlockSpec(memory_space=pltpu.SMEM)
HBM = pl.BlockSpec(memory_space=pltpu.HBM)


def dot(a, b, ca, cb):
    return lax.dot_general(a, b, (((ca,), (cb,)), ((), ())), preferred_element_type=jnp.float32)


def focus_kernel(lat_ref, ver_ref, echo_ref, kern_ref, *outs):
    _, passes, pulses, _ = echo_ref.shape
    cols = kern_ref.shape[2]
    far = len(outs)
    x = lax.axis_index("x")
    c = lax.axis_index("c")
    pairs = [(x + s) % far * 2 for s in range(far)]
    kr = kern_ref[0]
    ki = kern_ref[1]
    er, ei = (
        jnp.concatenate(
            [echo_ref[part, pl.ds(pair, 2)].reshape(2 * pulses, -1) for pair in pairs], axis=0
        )
        for part in range(2)
    )
    fr = dot(er, kr, 1, 0) - dot(ei, ki, 1, 0)
    fi = dot(er, ki, 1, 0) + dot(ei, kr, 1, 0)
    col = lax.broadcasted_iota(jnp.int32, (pulses, cols), 1)
    for s, out in enumerate(outs):
        for p in range(2):
            lag = lat_ref[pairs[s] + p]
            keep = col >= lag
            at = (2 * s + p) * pulses
            for part, value in enumerate((fr, fi)):
                moved = pltpu.roll(value[at : at + pulses], lag, 1)
                out[(c + p) % 2, part, 0:pulses] = jnp.where(keep, moved, 0.0).astype(out.dtype)
    extra = outs[0].shape[2] - pulses
    row_lag = jnp.full((extra, cols), ver_ref[pairs[0] + c].astype(jnp.float32))
    for k in range(2):
        for part in range(2):
            outs[0][k, part, pulses : pulses + extra] = row_lag.astype(outs[0].dtype)


def image_kernel(far, *refs):
    out_ref, out_mem, re_ref, im_ref, out_sem = refs[-5:]
    tables = list(refs[:-5])
    focus_refs = tables[-2 * far :]
    held = tables[: -2 * far]
    _, pulses, rows = held[0].shape
    cols = out_ref.shape[1]
    fr = jnp.concatenate([ref[i // far, 0, 0:pulses] for i, ref in enumerate(focus_refs)], axis=0)
    fi = jnp.concatenate([ref[i // far, 1, 0:pulses] for i, ref in enumerate(focus_refs)], axis=0)
    lag = jnp.max(focus_refs[0][0, 0, pulses:].astype(jnp.float32)).astype(jnp.int32)
    re_ref[0:ROW_MAX] = jnp.zeros((ROW_MAX, cols), jnp.float32)
    im_ref[0:ROW_MAX] = jnp.zeros((ROW_MAX, cols), jnp.float32)
    start = ROW_MAX - lag
    base = pl.multiple_of(start // 8 * 8, 8)
    rest = start - base
    step = 128
    sub = lax.broadcasted_iota(jnp.int32, (step // 8, 8, cols), 1)
    def planes(refs):
        mine, one, two_r, two_i, three = refs
        return (
            [mine.at[0], one.at[0], two_r, three.at[0]],
            [mine.at[1], one.at[1], two_i, three.at[1]],
        )

    own = planes(held[:5])
    sibling = planes(held[5:])
    real = own[0] + sibling[0]
    imag = own[1] + sibling[1]

    def product(r0):
        ar = jnp.concatenate([ref[:, r0 : r0 + step] for ref in real], axis=0)
        ai = jnp.concatenate([ref[:, r0 : r0 + step] for ref in imag], axis=0)
        return dot(ar, fr, 0, 0) - dot(ai, fi, 0, 0), dot(ar, fi, 0, 0) + dot(ai, fr, 0, 0)

    def keep(r0, value):
        re_ref[ROW_MAX + r0 : ROW_MAX + r0 + step] = value[0]
        im_ref[ROW_MAX + r0 : ROW_MAX + r0 + step] = value[1]

    def shifted(ref, r0):
        wide = ref[pl.ds(base + r0, step + 8)]
        return pltpu.roll(wide, step + 8 - rest, 0)[:step].reshape(step // 8, 8, cols)

    def copy(r0):
        piece = pl.ds(2 * r0, 2 * step)
        return pltpu.make_async_copy(out_mem.at[piece], out_ref.at[piece], out_sem.at[r0 // step])

    keep(0, product(0))
    for r0 in range(0, rows, step):
        last = r0 + step == rows
        value = None if last else product(r0 + step)
        re = shifted(re_ref, r0)
        im = shifted(im_ref, r0)
        first = jnp.where(sub < 4, re, pltpu.roll(im, 4, 1))
        second = jnp.where(sub < 4, pltpu.roll(re, 4, 1), im)
        both = jnp.stack([first, second], axis=1).reshape(2 * step, cols)
        out_mem[2 * r0 : 2 * r0 + 2 * step] = both.astype(out_mem.dtype)
        copy(r0).start()
        if not last:
            keep(r0 + step, value)
    for r0 in range(0, rows, step):
        copy(r0).wait()


def recover_kernel(img_ref, g_ref, h_ref, out_ref, y_ref, out_mem, out_sem):
    outer, parts, inner, eight, cols = img_ref.shape
    passes = outer * inner
    own = eight // 2
    for k in range(outer):
        acc = img_ref[k, 0].astype(jnp.float32)
        for z in range(1, parts):
            acc = acc + img_ref[k, z].astype(jnp.float32)
        acc = acc.reshape(inner * eight, cols)
        at = k * inner * eight
        for c in range(cols // 128):
            y_ref[c, at : at + inner * eight] = acc[:, c * 128 : c * 128 + 128]

    g = g_ref[...]
    h = h_ref[...]

    def shrink(v):
        return v - jnp.clip(v, -LEVEL, LEVEL)

    def copy(i, c):
        piece = pl.ds(c * 128, 128)
        return pltpu.make_async_copy(out_mem.at[:, i, piece], out_ref.at[:, i, piece], out_sem.at[i, c])

    for i in range(own):
        chains = []
        for c in range(cols // 128):
            re = y_ref.at[c][pl.ds(i, passes, stride=eight), :]
            im = y_ref.at[c][pl.ds(own + i, passes, stride=eight), :]
            y = jnp.concatenate([re, im], axis=0).T.astype(jnp.bfloat16)
            chains += [y[:64], y[64:]]
        wide = [y.astype(jnp.float32) for y in chains]
        us = [shrink(dot(y, g, 1, 0)) for y in chains]
        for _ in range(ITERS - 1):
            resids = [
                (y - dot(u.astype(jnp.bfloat16), h, 1, 0)).astype(jnp.bfloat16)
                for y, u in zip(wide, us)
            ]
            us = [shrink(u + dot(r, g, 1, 0)) for u, r in zip(us, resids)]
        for k, u in enumerate(us):
            out_mem[0, i, k * 64 : k * 64 + 64] = u[:, :BINS]
            out_mem[1, i, k * 64 : k * 64 + 64] = u[:, BINS:]
            if k % 2 == 1:
                copy(i, k // 2).start()
    for i in range(own):
        for c in range(cols // 128):
            copy(i, c).wait()


def steering(normal_spacings, source):
    chosen = jnp.sum(
        jnp.where(
            source[:, None] == jnp.arange(normal_spacings.shape[0], dtype=jnp.int32)[None, :],
            normal_spacings[None, :],
            0.0,
        ),
        axis=1,
    )
    bins = jnp.arange(BINS).astype(normal_spacings.dtype) - BINS // 2
    phases = jnp.pi * chosen[:, None] * bins[None, :]
    return jnp.cos(phases), jnp.sin(phases)


def partial_image(echo, along, slant, vertical, lateral):
    passes = vertical.shape[0]
    pulses = along.shape[2]
    rows = along.shape[1]
    freqs, cols = slant.shape[1:]
    bf = jnp.bfloat16
    nx = lax.axis_size("x")

    def turn(value, step):
        return lax.ppermute(value, "x", [(i, (i + step) % nx) for i in range(nx)])

    def swap(value):
        return lax.ppermute(value, "c", [(0, 1), (1, 0)])

    at = jnp.transpose(along, (0, 2, 1))
    one = turn(at, 1)
    three = turn(at, 3)
    pass_re, pass_im = one[0], three[1]
    two_re = turn(pass_re, 1)
    two_im = turn(pass_im, 3)

    spare = 16
    shapes = [(2, 2, pulses + spare, cols)] + [(2, 2, pulses, cols)] * (nx - 1)
    focus = pl.pallas_call(
        focus_kernel,
        out_shape=[jax.ShapeDtypeStruct(shape, bf) for shape in shapes],
        in_specs=[SMEM, SMEM, VMEM, VMEM],
        out_specs=[VMEM] * nx,
        name="focus",
    )(lateral, vertical, echo, slant)
    focus = [focus[0]] + [turn(focus[s], s) for s in range(1, nx)]
    inside = lax.axis_index("x") < nx
    at_here, focus_here, _, _ = lax.optimization_barrier((at, focus[0], pass_re, pass_im))
    own = jnp.where(inside, at_here, jnp.zeros_like(at))
    own_focus = jnp.where(inside, focus_here, jnp.zeros_like(focus[0]))
    at_late, one_late, three_late, own, own_focus, *focus = lax.optimization_barrier(
        (at, one, three, own, own_focus, *focus)
    )
    focus = focus + [swap(value) for value in focus]
    held = [one, two_re, two_im, three]
    swapped = [swap(value) for value in (at_late, one_late, two_re, two_im, three_late)]
    focus[0] = own_focus
    held = [own] + held + swapped
    return pl.pallas_call(
        functools.partial(image_kernel, nx),
        out_shape=jax.ShapeDtypeStruct((2 * rows, cols), bf),
        in_specs=[VMEM] * (len(held) + len(focus)),
        out_specs=HBM,
        scratch_shapes=[
            pltpu.VMEM((2 * rows, cols), bf),
            pltpu.VMEM((rows + ROW_MAX + 8, cols), jnp.float32),
            pltpu.VMEM((rows + ROW_MAX + 8, cols), jnp.float32),
            pltpu.SemaphoreType.DMA((rows // 128,)),
        ],
        compiler_params=pltpu.CompilerParams(vmem_limit_bytes=40 << 20),
        name="image",
    )(*held, *focus)


def body(echo, along, slant, vertical, lateral, survey, spacings):
    total = survey.shape[0]
    cols = slant.shape[2]
    bf = jnp.bfloat16
    nx, nz, nc, ny, nl = (lax.axis_size(name) for name in ("x", "zh", "c", "y", "zl"))
    image = partial_image(echo, along, slant, vertical, lateral)
    image = lax.all_to_all(image, ("x", "zh", "c", "y", "zl"), 0, 0, tiled=True)

    source = survey.reshape(ny * nl, nx * nc).T.reshape(total)
    cos, sin = steering(spacings, source)
    g = jnp.concatenate(
        [jnp.concatenate([cos, -sin], axis=1), jnp.concatenate([sin, cos], axis=1)], axis=0
    )
    gb = (g / total).astype(bf)
    hb = (g.T / BINS).astype(bf)
    own = 4
    image = image.reshape(nx, nz, nc * ny * nl, 2 * own, cols)
    return pl.pallas_call(
        recover_kernel,
        out_shape=jax.ShapeDtypeStruct((2, own, cols, BINS), jnp.float32),
        in_specs=[VMEM] * 3,
        out_specs=HBM,
        scratch_shapes=[
            pltpu.VMEM((cols // 128, total * 2 * own, 128), jnp.float32),
            pltpu.VMEM((2, own, cols, BINS), jnp.float32),
            pltpu.SemaphoreType.DMA((own, cols // 128)),
        ],
        compiler_params=pltpu.CompilerParams(vmem_limit_bytes=40 << 20),
        name="recover",
    )(image, gb, hb)


def solution(mesh):
    fine = Mesh(mesh.devices.reshape(4, 4, 2, 4, 2), ("x", "zh", "c", "y", "zl"))
    ap = ("x", "zh", "c")
    group = ("y", "zl")
    return jax.shard_map(
        body,
        mesh=fine,
        in_specs=(
            P(None, group, ap, None),
            P(None, None, ap),
            P(),
            P(group),
            P(group),
            P(),
            P(),
        ),
        out_specs=P(None, ap + group, None, None),
        check_vma=False,
    )
```
